32 devices in a mesh: group: 2 (over y), gx: 4 (over x, core), gy: 4 (over z).
Axes of the slice: x: 2, y: 2, z: 4, core: 2. Of those that a mesh axis runs over, the one named last changes fastest.
Arguments:
- pressure: float32 [192, 64, 768], P(('group', 'gx'), 'gy'), parts along dimension 0, may hold values from -6 to 6
- pressure_prev: float32 [192, 64, 768], P(('group', 'gx'), 'gy'), parts along dimension 0, may hold values from -6 to 6
- courant: float32 [192, 64, 768], P(('group', 'gx'), 'gy'), parts along dimension 0, may hold values from 0.05 to 0.3
- nonlinearity: float32 [192, 64, 768], P(('group', 'gx'), 'gy'), parts along dimension 0, may hold values from 0.03 to 0.3
- absorption: float32 [192, 64, 768], P(('group', 'gx'), 'gy'), parts along dimension 0, may hold values from 0.2 to 2
- own_map: int32 [96, 32], P(('group', 'gx'), 'gy'), parts along dimension 0, may hold values from 0 to 16, as said below
- slot_table: int32 [96, 32], P(('group', 'gx'), 'gy'), parts along dimension 0, may hold values from 0 to 511
- displacement: float32 [128, 128, 384], P(('group', 'gx'), 'gy'), parts along dimension 0, may hold values from -6 to 6
- displacement_prev: float32 [128, 128, 384], P(('group', 'gx'), 'gy'), parts along dimension 0, may hold values from -6 to 6
- layer_labels: int32 [128, 128, 384], P(('group', 'gx'), 'gy'), parts along dimension 0, may hold values from 0 to 3
- shear_table: float32 [8], P('group'), parts along dimension 0, may hold values from 0.05 to 0.15
- viscosity_table: float32 [8], P('group'), parts along dimension 0, may hold values from 0.01 to 0.06
Outputs:
- pressure_mid: float32 [192, 64, 768], P(('group', 'gx'), 'gy'), parts along dimension 0
- pressure_new: float32 [192, 64, 768], P(('group', 'gx'), 'gy'), parts along dimension 0
- tissue_force: float32 [128, 128, 384], P(('group', 'gx'), 'gy'), parts along dimension 0
- displacement_mid: float32 [128, 128, 384], P(('group', 'gx'), 'gy'), parts along dimension 0
- displacement_new: float32 [128, 128, 384], P(('group', 'gx'), 'gy'), parts along dimension 0
The draws below stay inside these ranges and needn't reach their ends.
There are 2 independent parts, one for each index of `group`. The reference program is written for one: setup_inputs(seed, part) draws one part's arguments, and reference() takes and returns one part's arrays. A program takes and returns all parts, laid end to end along the dimension named above; each array names one. Nothing has to cross between parts.
Inputs may be any that keep to these rules, and one draw needn't show every extreme that they name: `own_map`: A value below 16 names tissue block (v // 4, v % 4); 16 marks a line outside the focal zone. Among the lines of one device's block of the map, at most 6 name any one tissue block, and exactly 6 do for some block in every draw.
All inputs are finite; a program needn't handle non-finite values.
Results may differ from the reference program's by a relative error of at most 0.0003.
Values sent between devices are 32-bit elements; how exact they have to be, the bound alone decides.
No kernel may reach another device: no remote copies, remote signals or barrier semaphores. Data moves between devices by JAX's collectives and lax.ppermute only.
A program may use at most 64 MiB of HBM per device.

```python
import math
import jax
import jax.numpy as jnp
from jax import lax

BZ = 24
CX = 16
NY = 768
RX = 16
RY = 32
LAYERS = 4
TZ = 384
NZ = 96
NX = 64
TX = 64
TY = 128
TROWS = 4
TCOLS = 4
TILES = 16
CAP = 6


def focal_routing(key):
    keys = jax.random.split(jax.random.fold_in(key, 7), 2)
    outside_row = jax.random.randint(keys[0], (), 0, TROWS)
    offsets = jax.random.randint(keys[1], (TILES,), 0, TILES)
    depth = BZ // 2
    across = CX // 2
    line_z = jnp.arange(NZ // 2, dtype=jnp.int32)[:, None]
    line_x = jnp.arange(NX // 2, dtype=jnp.int32)[None, :]
    source_row = line_z // depth
    source_col = line_x // across
    local = line_z % depth * across + line_x % across
    group_index = local // CAP
    source = source_row * TCOLS + source_col
    focal = source_row != outside_row
    target = (offsets[source] + group_index) % TILES
    return jnp.where(focal, target, TILES).astype(jnp.int32)


def draw_own_map(key, part):
    return focal_routing(key)


def plant(array, rng, least, high):
    longest = array.shape.index(max(array.shape))
    spots = []
    for shift in (0, 1):
        where = [jax.random.randint(jax.random.fold_in(rng, axis), (), 0, length) for axis, length in enumerate(array.shape)]
        where[longest] = (where[longest] + shift) % array.shape[longest]
        spots.append(tuple(where))
    return array.at[spots[0]].set(least).at[spots[1]].set(high)


def level_of(own_key, dims, cuts, least, largest):
    loudness, own = 1.0, jax.random.fold_in(own_key, 6)
    for position, blocks in cuts:
        draws = jnp.exp(jax.random.uniform(jax.random.fold_in(own, position), (blocks,), jnp.float32, least / len(cuts), largest / len(cuts)))
        loudness = loudness * jnp.repeat(draws, dims[position] // blocks).reshape([-1 if axis == position else 1 for axis in range(len(dims))])
    return loudness


def scatter_about(own_key, shape, deviation, most, cuts=(), kind=jnp.bfloat16):
    entries = deviation * jax.random.normal(own_key, shape, jnp.float32)
    if cuts:
        entries = entries * level_of(own_key, shape, cuts, -0.22, 0.18)
    return jnp.clip(entries, -most, most).astype(kind)


def setup_inputs(seed: int = 0, part: int = 0) -> dict:
    key_of = jax.random.split(jax.random.key(seed), 13)
    part_keys = jax.random.split(jax.random.fold_in(key_of[12], part), 13)
    pressure = scatter_about(part_keys[0], (NZ, NX, NY), 1.0, 6.0, ((0, 4), (1, 4)), jnp.float32)
    pressure_prev = scatter_about(part_keys[1], (NZ, NX, NY), 1.0, 6.0, ((0, 4), (1, 4)), jnp.float32)
    courant = jnp.clip(jnp.exp(math.log(0.3) - 1.7917595 * jax.random.uniform(part_keys[2], (NZ, NX, NY), jnp.float32) ** level_of(part_keys[2], (NZ, NX, NY), ((0, 4), (1, 4)), -0.2, 0.2)), 0.05, 0.3)
    nonlinearity = jnp.clip(jnp.exp(math.log(0.3) - 2.3025852 * jax.random.uniform(part_keys[3], (NZ, NX, NY), jnp.float32) ** level_of(part_keys[3], (NZ, NX, NY), ((0, 4), (1, 4)), -0.2, 0.2)), 0.03, 0.3)
    absorption = jnp.clip(jnp.exp(math.log(2.0) - 2.3025851 * jax.random.uniform(part_keys[4], (NZ, NX, NY), jnp.float32) ** level_of(part_keys[4], (NZ, NX, NY), ((0, 4), (1, 4)), -0.2, 0.2)), 0.2, 2.0)
    own_map = draw_own_map(jax.random.fold_in(jax.random.fold_in(key_of[12], part), 71), part)
    slot_table = plant(jax.random.randint(part_keys[6], (NZ // 2, NX // 2), 0, RX * RY), jax.random.fold_in(part_keys[6], 1), 0, (RX * RY) - 1).astype(jnp.int32)
    displacement = scatter_about(part_keys[7], (TX, TY, TZ), 1.0, 6.0, ((0, 4), (1, 4)), jnp.float32)
    displacement_prev = scatter_about(part_keys[8], (TX, TY, TZ), 1.0, 6.0, ((0, 4), (1, 4)), jnp.float32)
    layer_labels = plant(jax.random.randint(part_keys[9], (TX, TY, TZ), 0, LAYERS), jax.random.fold_in(part_keys[9], 1), 0, LAYERS - 1).astype(jnp.int32)
    shear_table = jnp.clip(jnp.exp(jax.random.uniform(part_keys[10], (LAYERS,), jnp.float32, math.log(0.05), math.log(0.15))), 0.05, 0.15)
    viscosity_table = jnp.clip(jnp.exp(jax.random.uniform(part_keys[11], (LAYERS,), jnp.float32, math.log(0.01), math.log(0.06))), 0.01, 0.06)
    return dict(pressure=pressure, pressure_prev=pressure_prev, courant=courant, nonlinearity=nonlinearity, absorption=absorption, own_map=own_map, slot_table=slot_table, displacement=displacement, displacement_prev=displacement_prev, layer_labels=layer_labels, shear_table=shear_table, viscosity_table=viscosity_table)


def laplace_pad(field):
    padded = jnp.pad(field, 1)
    total = padded[2:, 1:-1, 1:-1] + padded[:-2, 1:-1, 1:-1]
    total = total + padded[1:-1, 2:, 1:-1] + padded[1:-1, :-2, 1:-1]
    total = total + padded[1:-1, 1:-1, 2:] + padded[1:-1, 1:-1, :-2]
    return total - 6.0 * field

def acoustic_step(now, before, courant, nonlinearity, absorption):
    return 2.0 * now - before + courant * laplace_pad(now) + nonlinearity * (now * now - before * before) - 0.1 * absorption * (now - before)

def layer_lookup(labels, table):
    result = jnp.zeros(labels.shape, jnp.float32)
    for kind in range(table.shape[0]):
        result = result + jnp.where(labels == kind, table[kind], 0.0)
    return result

def reference(pressure, pressure_prev, courant, nonlinearity, absorption, own_map, slot_table, displacement, displacement_prev, layer_labels, shear_table, viscosity_table):
    pressure_mid = acoustic_step(pressure, pressure_prev, courant, nonlinearity, absorption)
    pressure_new = acoustic_step(pressure_mid, pressure, courant, nonlinearity, absorption)
    force = 0.1 * absorption * (pressure_mid * pressure_mid + pressure_new * pressure_new) * lax.rsqrt(courant)
    coarse = force.reshape(NZ // 2, 2, NX // 2, 2, TZ, 2).sum(axis=(1, 3, 5)) * 0.125
    rows = own_map // TCOLS * RX + slot_table // RY
    cols = own_map % TCOLS * RY + slot_table % RY
    target = jnp.where(own_map < TILES, rows * TY + cols, TX * TY).astype(jnp.int32)
    summed = jax.ops.segment_sum(coarse.reshape(-1, TZ), target.reshape(-1), num_segments=TX * TY + 1)
    tissue_force = summed[:-1].reshape(TX, TY, TZ)
    shear = layer_lookup(layer_labels, shear_table)
    viscosity = layer_lookup(layer_labels, viscosity_table)

    def elastic_step(now, before):
        return 2.0 * now - before + shear * laplace_pad(now) + viscosity * laplace_pad(now - before) + 0.25 * tissue_force
    displacement_mid = elastic_step(displacement, displacement_prev)
    displacement_new = elastic_step(displacement_mid, displacement)
    return (pressure_mid, pressure_new, tissue_force, displacement_mid, displacement_new)
```

```python
import functools

import jax
import jax.numpy as jnp
from jax import lax
from jax.experimental import pallas as pl
from jax.experimental.pallas import tpu as pltpu
from jax.sharding import PartitionSpec as P

VMEM = pl.BlockSpec(memory_space=pltpu.VMEM)
SMEM = pl.BlockSpec(memory_space=pltpu.SMEM)
EXACT = lax.Precision.HIGHEST


def lateral(x):
    dim, size = x.ndim - 1, x.shape[-1]
    lane = lax.broadcasted_iota(jnp.int32, x.shape, dim)
    lower = jnp.where(lane == 0, 0.0, pltpu.roll(x, 1, dim))
    upper = jnp.where(lane == size - 1, 0.0, pltpu.roll(x, size - 1, dim))
    return lower + upper


def beside(x, before, after):
    size = x.shape[0]
    row = lax.broadcasted_iota(jnp.int32, x.shape, 0)
    up = jnp.where(row == 0, before, pltpu.roll(x, 1, 0))
    down = jnp.where(row == size - 1, after, pltpu.roll(x, size - 1, 0))
    return up + down


def at_ends(shape, first, last):
    row = lax.broadcasted_iota(jnp.int32, shape, 0)
    return jnp.where(row == 0, first, jnp.where(row == shape[0] - 1, last, 0.0))


def wave(now, before, lap, courant, nonlinearity, absorption):
    return (
        2.0 * now
        - before
        + courant * lap
        + nonlinearity * (now * now - before * before)
        - 0.1 * absorption * (now - before)
    )


def lookup(kinds, table, first):
    result = jnp.zeros(kinds.shape, jnp.float32)
    for kind in range(table.shape[0]):
        result = jnp.where(kinds == kind + first, table[kind], result)
    return result


def halves(ref, base, x):
    half, depth = x.shape[0] // 2, x.shape[1]
    ref[base : base + half, 0:depth] = x[:half]
    ref[base : base + half, depth : 2 * depth] = x[half:]


def whole(ref, base, half, depth):
    return jnp.concatenate(
        [ref[base : base + half, 0:depth], ref[base : base + half, depth : 2 * depth]], axis=0
    )


def border_rows(*refs):
    fields, (shear, viscosity, first, last), buffers, sems = refs[:8], refs[8:12], refs[12:28], refs[28]
    copies = []
    for k, buffer in enumerate(buffers):
        field, count = fields[k // 2], buffer.shape[0]
        start = 0 if k % 2 == 0 else field.shape[0] - count
        copies.append(
            pltpu.make_async_copy(field.at[pl.ds(start, count)], buffer, sems.at[k])
        )
    for copy in copies:
        copy.start()
    for copy in copies:
        copy.wait()
    p0, p1, q0, q1, c0, c1, n0, n1, a0, a1, d0, d1, e0, e1, l0, l1 = buffers
    sides = (
        (p0, 0, 1, q0, c0, n0, a0, d0, e0, l0, first),
        (p1, 1, 0, q1, c1, n1, a1, d1, e1, l1, last),
    )
    for p_ref, at, inner, q_ref, c_ref, n_ref, a_ref, d_ref, b_ref, l_ref, out in sides:
        p, c = p_ref[at], c_ref[0]
        across, half = p.shape[0], d_ref.shape[1] // 2
        lap = p_ref[inner] + beside(p, 0.0, 0.0) + lateral(p) - 6.0 * p
        out[0:across] = p
        out[across : 2 * across] = c
        out[2 * across : 3 * across] = wave(p, q_ref[0], lap, c, n_ref[0], a_ref[0])
        d = d_ref[at]
        e = d - b_ref[at]
        d_in = d_ref[inner]
        e_in = d_in - b_ref[inner]
        labels = l_ref[0]
        s, v = lookup(labels, shear, 0), lookup(labels, viscosity, 0)
        lap_d = d_in + beside(d, 0.0, 0.0) + lateral(d) - 6.0 * d
        lap_e = e_in + beside(e, 0.0, 0.0) + lateral(e) - 6.0 * e
        base = 3 * across
        halves(out, base, d)
        halves(out, base + half, e)
        halves(out, base + 2 * half, d + e + s * lap_d + v * lap_e)
        halves(out, base + 3 * half, labels.astype(jnp.float32) + 1.0)


def border_columns(
    p_ref, q_ref, c_ref, n_ref, a_ref, d_ref, b_ref, l_ref, shear, viscosity, before, after, left, right
):
    deep, across, _ = p_ref.shape
    rows, cols, depth = d_ref.shape
    half = cols // 2
    row = lambda ref, base, j: ref[base + j : base + j + 1, :]
    base = 3 * across

    def line(ref, offset, j):
        at, lane = (j, 0) if j < half else (j - half, depth)
        return ref[base + offset + at : base + offset + at + 1, lane : lane + depth]

    for j, inner, k, k_in, out in (
        (0, 1, 0, 1, left),
        (across - 1, across - 2, cols - 1, cols - 2, right),
    ):
        p, c = p_ref[:, j, :], c_ref[:, j, :]
        p_up, p_down = row(before, 0, j), row(after, 0, j)
        lap = beside(p, p_up, p_down) + p_ref[:, inner, :] + lateral(p) - 6.0 * p
        out[0:deep] = p
        out[deep : 2 * deep] = c
        out[2 * deep : 3 * deep] = wave(
            p, q_ref[:, j, :], lap, c, n_ref[:, j, :], a_ref[:, j, :]
        )
        d = d_ref[:, k, :]
        e = d - b_ref[:, k, :]
        d_in = d_ref[:, k_in, :]
        e_in = d_in - b_ref[:, k_in, :]
        labels = l_ref[:, k, :]
        s, v = lookup(labels, shear, 0), lookup(labels, viscosity, 0)
        d_up, d_down = line(before, 0, k), line(after, 0, k)
        e_up, e_down = line(before, half, k), line(after, half, k)
        lap_d = beside(d, d_up, d_down) + d_in + lateral(d) - 6.0 * d
        lap_e = beside(e, e_up, e_down) + e_in + lateral(e) - 6.0 * e
        top = 3 * deep
        out[top : top + 1] = p_up
        out[top + 1 : top + 2] = p_down
        out[top + 2 : top + 3, 0:depth] = d_up
        out[top + 2 : top + 3, depth : 2 * depth] = e_up
        out[top + 3 : top + 4, 0:depth] = d_down
        out[top + 3 : top + 4, depth : 2 * depth] = e_down
        out[top + 4 : top + 8] = jnp.zeros((4, p.shape[1]), jnp.float32)
        out[top + 8 : top + 8 + rows, 0:depth] = d
        out[top + 8 : top + 8 + rows, depth : 2 * depth] = e
        out[top + 8 + rows : top + 8 + 2 * rows, 0:depth] = labels.astype(jnp.float32) + 1.0
        out[top + 8 + rows : top + 8 + 2 * rows, depth : 2 * depth] = (
            d + e + s * lap_d + v * lap_e
        )


def first_steps(
    p_ref, q_ref, c_ref, n_ref, a_ref, d_ref, b_ref, l_ref, shear, viscosity, before, after, mid, free
):
    deep, across, _ = p_ref.shape
    rows, cols, depth = d_ref.shape
    half = cols // 2
    base = 3 * across

    def acoustic(i, p_up, p_down):
        p = p_ref[i]
        lap = p_up + p_down + beside(p, 0.0, 0.0) + lateral(p) - 6.0 * p
        mid[i] = wave(p, q_ref[i], lap, c_ref[i], n_ref[i], a_ref[i])

    acoustic(0, before[0:across], p_ref[1])
    acoustic(deep - 1, p_ref[deep - 2], after[0:across])

    def acoustic_body(i, carry):
        acoustic(i, p_ref[i - 1], p_ref[i + 1])
        return carry

    lax.fori_loop(1, deep - 1, acoustic_body, 0)

    def elastic(i, d_up, d_down, e_up, e_down):
        d = d_ref[i]
        e = d - b_ref[i]
        s, v = lookup(l_ref[i], shear, 0), lookup(l_ref[i], viscosity, 0)
        lap_d = d_up + d_down + beside(d, 0.0, 0.0) + lateral(d) - 6.0 * d
        lap_e = e_up + e_down + beside(e, 0.0, 0.0) + lateral(e) - 6.0 * e
        free[i] = d + e + s * lap_d + v * lap_e

    change = lambda i: d_ref[i] - b_ref[i]
    elastic(
        0, whole(before, base, half, depth), d_ref[1], whole(before, base + half, half, depth), change(1)
    )
    elastic(
        rows - 1,
        d_ref[rows - 2],
        whole(after, base, half, depth),
        change(rows - 2),
        whole(after, base + half, half, depth),
    )

    def elastic_body(i, carry):
        elastic(i, d_ref[i - 1], d_ref[i + 1], change(i - 1), change(i + 1))
        return carry

    lax.fori_loop(1, rows - 1, elastic_body, 0)


def dot(x, y, contract=((1,), (0,))):
    return lax.dot_general(
        x, y, (contract, ((), ())), precision=EXACT, preferred_element_type=jnp.float32
    )


def selected(x, y):
    high = y.astype(jnp.bfloat16)
    low = (y - high.astype(jnp.float32)).astype(jnp.bfloat16)
    x = x.astype(jnp.bfloat16)
    product = functools.partial(jnp.dot, preferred_element_type=jnp.float32)
    return product(x, high) + product(x, low)


def iota(shape, dim):
    return lax.broadcasted_iota(jnp.int32, shape, dim)


def second_acoustic(
    blocks,
    capacity,
    chunk,
    mid_ref,
    p_ref,
    c_ref,
    n_ref,
    a_ref,
    own_ref,
    slot_ref,
    before,
    after,
    left,
    right,
    mid,
    new,
    send,
    first_col,
    last_col,
    pairs,
):
    deep, across, span = p_ref.shape
    mid[...] = mid_ref[...]
    for j, side, beyond in ((0, left, first_col), (across - 1, right, last_col)):
        mid[:, j, :] = mid_ref[:, j, :] + c_ref[:, j, :] * side[0:deep]
        beyond[...] = side[2 * deep : 3 * deep] + side[deep : 2 * deep] * p_ref[:, j, :]
    top = 3 * deep

    def row_beyond(side, edge, k):
        c = side[across : 2 * across]
        corners = at_ends(c.shape, left[top + k : top + k + 1], right[top + k : top + k + 1])
        return side[2 * across : 3 * across] + c * (p_ref[edge] + corners)

    def step(i, up, down):
        m, p, c, a = mid[i], p_ref[i], c_ref[i], a_ref[i]
        sides = beside(m, first_col[pl.ds(i, 1), :], last_col[pl.ds(i, 1), :])
        lap = up + down + sides + lateral(m) - 6.0 * m
        result = wave(m, p, lap, c, n_ref[i], a)
        new[i] = result
        return 0.1 * a * (m * m + result * result) * lax.rsqrt(c)

    def put(k, value):
        at = pl.ds(pl.multiple_of(k * across, across), across)
        for part in range(span // 128):
            pairs[part, at, :] = value[:, part * 128 : part * 128 + 128]

    put(0, step(0, row_beyond(before, 0, 0), mid[1]) + step(1, mid[0], mid[2]))
    put(
        deep // 2 - 1,
        step(deep - 2, mid[deep - 3], mid[deep - 1])
        + step(deep - 1, mid[deep - 2], row_beyond(after, deep - 1, 1)),
    )

    def body(k, carry):
        i = 2 * k
        put(k, step(i, mid[i - 1], mid[i + 1]) + step(i + 1, mid[i], mid[i + 2]))
        return carry

    lax.fori_loop(1, deep // 2 - 1, body, 0)
    count = deep // 2 * (across // 2)
    paired = jnp.concatenate(
        [
            pairs[part, pl.ds(0, count, stride=2), :] + pairs[part, pl.ds(1, count, stride=2), :]
            for part in range(span // 128)
        ],
        axis=1,
    )
    pairing = iota((256, 128), 0) // 2 == iota((256, 128), 1)
    pairing = pairing.astype(jnp.float32).astype(jnp.bfloat16)
    high = paired.astype(jnp.bfloat16)
    low = (paired - high.astype(jnp.float32)).astype(jnp.bfloat16)
    product = functools.partial(jnp.dot, preferred_element_type=jnp.float32)
    lines = 0.125 * jnp.concatenate(
        [
            product(high[:, at : at + 256], pairing) + product(low[:, at : at + 256], pairing)
            for at in range(0, span, 256)
        ],
        axis=1,
    )
    wide, tall = own_ref.shape
    spread = (iota((tall, count), 1) // wide == iota((tall, count), 0)).astype(jnp.float32)
    mine = iota((wide, count), 1) % wide == iota((wide, count), 0)
    spread_t = (iota((count, tall), 0) // wide == iota((count, tall), 1)).astype(jnp.float32)
    mine_t = iota((count, wide), 0) % wide == iota((count, wide), 1)

    def flat(ref):
        x = ref[...].astype(jnp.float32)
        along = jnp.sum(jnp.where(mine, dot(x, spread), 0.0), axis=0, keepdims=True)
        down = dot(spread_t, x, ((1,), (1,)))
        return along, jnp.sum(jnp.where(mine_t, down, 0.0), axis=1, keepdims=True)

    own_row, own_col = flat(own_ref)
    _, slot_col = flat(slot_ref)
    same = own_row == own_col
    before_it = iota((count, count), 0) < iota((count, count), 1)
    after_it = iota((count, count), 0) > iota((count, count), 1)
    ones = lambda x: jnp.where(x, 1.0, 0.0)
    rank_row = jnp.sum(ones(same & before_it), axis=0, keepdims=True)
    rank_col = jnp.sum(ones(same & after_it), axis=1, keepdims=True)
    total = blocks * chunk
    at = iota((total, count), 0)
    owner = own_row.astype(jnp.int32)
    match = ones(at == owner * chunk + rank_row.astype(jnp.int32))
    placing = ones(at == owner * chunk + capacity)
    depth = lines.shape[1]
    places = jnp.where(iota((count, depth), 1) == rank_col.astype(jnp.int32), slot_col + 1.0, 0.0)
    send[...] = selected(match, lines) + selected(placing, places)


def second_elastic(
    free_ref, d_ref, b_ref, l_ref, shear, viscosity, before, after, left, right, free, after_free,
    d_first, d_last, f_first, f_last
):
    rows, cols, depth = d_ref.shape
    half = cols // 2
    across = (before.shape[0] - 2 * cols) // 3
    base = 3 * across
    top = left.shape[0] - 2 * rows - 8
    free[...] = free_ref[...]
    for j, side, d_col, f_col in ((0, left, d_first, f_first), (cols - 1, right, d_last, f_last)):
        labels = l_ref[:, j, :]
        s, v = lookup(labels, shear, 0), lookup(labels, viscosity, 0)
        d_side = side[top + 8 : top + 8 + rows, 0:depth]
        e_side = side[top + 8 : top + 8 + rows, depth : 2 * depth]
        free[:, j, :] = free_ref[:, j, :] + s * d_side + v * e_side
        kinds = side[top + 8 + rows : top + 8 + 2 * rows, 0:depth]
        s, v = lookup(kinds, shear, 1.0), lookup(kinds, viscosity, 1.0)
        d = d_ref[:, j, :]
        d_col[...] = d_side
        f_col[...] = (
            side[top + 8 + rows : top + 8 + 2 * rows, depth : 2 * depth]
            + s * d
            + v * (d - b_ref[:, j, :])
        )

    def beyond(side, edge, k):
        part = lambda n: whole(side, base + n * half, half, depth)
        d, kinds = part(0), part(3)
        s, v = lookup(kinds, shear, 1.0), lookup(kinds, viscosity, 1.0)
        d_edge = d_ref[edge]
        corner = lambda ref, lane: ref[top + k : top + k + 1, lane : lane + depth]
        d_ends = at_ends(d.shape, corner(left, 0), corner(right, 0))
        e_ends = at_ends(d.shape, corner(left, depth), corner(right, depth))
        f = part(2) + s * (d_edge + d_ends) + v * (d_edge - b_ref[edge] + e_ends)
        return f, d

    def step(i, f_up, f_down, d_up, d_down):
        f, d = free[i], d_ref[i]
        s, v = lookup(l_ref[i], shear, 0), lookup(l_ref[i], viscosity, 0)
        at = lambda ref: ref[pl.ds(i, 1), :]
        lap_f = f_up + f_down + beside(f, at(f_first), at(f_last)) + lateral(f) - 6.0 * f
        lap_d = d_up + d_down + beside(d, at(d_first), at(d_last)) + lateral(d) - 6.0 * d
        after_free[i] = 2.0 * f - d + s * lap_f + v * (lap_f - lap_d)

    f_up, d_up = beyond(before, 0, 2)
    step(0, f_up, free[1], d_up, d_ref[1])
    f_down, d_down = beyond(after, rows - 1, 3)
    step(rows - 1, free[rows - 2], f_down, d_ref[rows - 2], d_down)

    def body(i, carry):
        step(i, free[i - 1], free[i + 1], d_ref[i - 1], d_ref[i + 1])
        return carry

    lax.fori_loop(1, rows - 1, body, 0)


def land(capacity, chunk, got_ref, force):
    total, depth = got_ref.shape
    got = got_ref[...]
    pick = iota((total, total), 1) // chunk * chunk + capacity == iota((total, total), 0)
    lanes = dot(got[:, 0:128], jnp.where(pick, 1.0, 0.0), ((0,), (0,)))
    mine = iota(lanes.shape, 1) % chunk == iota(lanes.shape, 0)
    place = jnp.sum(jnp.where(mine, lanes, 0.0), axis=0, keepdims=True)
    rows, cols, _ = force.shape
    cells = rows * cols
    landing = jnp.where(iota((cells, total), 0) + 1 == place.astype(jnp.int32), 1.0, 0.0)
    force[...] = selected(landing, got).reshape(rows, cols, depth)


def last_steps(force, free, after_free, l_ref, shear, viscosity, up, down, left, right, mid, new):
    rows, cols, depth = force.shape

    def step(i, f_up, f_down):
        f = force[i]
        s, v = lookup(l_ref[i], shear, 0), lookup(l_ref[i], viscosity, 0)
        at = lambda ref: ref[pl.ds(i, 1), :]
        lap = f_up + f_down + beside(f, at(left), at(right)) + lateral(f) - 6.0 * f
        mid[i] = free[i] + 0.25 * f
        new[i] = after_free[i] + 0.75 * f + 0.25 * (s + v) * lap

    step(0, up[...], force[1])
    step(rows - 1, force[rows - 2], down[...])

    def body(i, carry):
        step(i, force[i - 1], force[i + 1])
        return carry

    lax.fori_loop(1, rows - 1, body, 0)


def swap(first, last, axis):
    size = lax.axis_size(axis)
    up = [(i, i + 1) for i in range(size - 1)]
    down = [(j, i) for i, j in up]
    return lax.ppermute(last, axis, up), lax.ppermute(first, axis, down)


def local(
    pressure,
    pressure_prev,
    courant,
    nonlinearity,
    absorption,
    own_map,
    slot_table,
    displacement,
    displacement_prev,
    layer_labels,
    shear_table,
    viscosity_table,
):
    deep, across, span = pressure.shape
    rows, cols, depth = displacement.shape
    f32 = lambda *shape: jax.ShapeDtypeStruct(shape, jnp.float32)
    params = pltpu.CompilerParams(vmem_limit_bytes=8 << 20)
    scratch = lambda *shape: pltpu.VMEM(shape, jnp.float32)

    def run(kernel, out, *args, scratch_shapes=(), tables=()):
        specs = [SMEM if k in tables else VMEM for k in range(len(args))]
        moved = 4 * sum(x.size for x in args) + 4 * sum(x.size for x in jax.tree.leaves(out))
        cost = pl.CostEstimate(flops=20 * moved, bytes_accessed=moved, transcendentals=0)
        return pl.pallas_call(
            kernel,
            out_shape=out,
            in_specs=specs,
            out_specs=jax.tree.map(lambda _: VMEM, out),
            scratch_shapes=scratch_shapes,
            compiler_params=params,
            cost_estimate=cost,
        )(*args)

    fields = (
        (pressure, 2),
        (pressure_prev, 1),
        (courant, 1),
        (nonlinearity, 1),
        (absorption, 1),
        (displacement, 2),
        (displacement_prev, 2),
        (layer_labels, 1),
    )
    face = 3 * across + 2 * cols
    first, last = pl.pallas_call(
        border_rows,
        out_shape=(f32(face, span), f32(face, span)),
        in_specs=[pl.BlockSpec(memory_space=pltpu.HBM)] * len(fields) + [SMEM, SMEM],
        out_specs=(VMEM, VMEM),
        scratch_shapes=[
            pltpu.VMEM((count,) + x.shape[1:], x.dtype) for x, count in fields for _ in range(2)
        ]
        + [pltpu.SemaphoreType.DMA((2 * len(fields),))],
        compiler_params=pltpu.CompilerParams(vmem_limit_bytes=55 << 20),
    )(*[x for x, _ in fields], shear_table, viscosity_table)
    before, after = swap(first, last, "gx")
    inputs = tuple(x for x, _ in fields) + (shear_table, viscosity_table, before, after)
    side = 3 * deep + 8 + 2 * rows
    first, last = run(border_columns, (f32(side, span),) * 2, *inputs, tables=(8, 9))
    left, right = swap(first, last, "gy")
    mid, free = run(
        first_steps, (f32(deep, across, span), f32(rows, cols, depth)), *inputs, tables=(8, 9)
    )
    blocks = lax.axis_size("gx") * lax.axis_size("gy")
    capacity = max(2, deep // 2 * (across // 2) // blocks)
    chunk = -(-(capacity + 1) // 8) * 8
    pressure_mid, pressure_new, send = run(
        functools.partial(second_acoustic, blocks, capacity, chunk),
        (f32(deep, across, span), f32(deep, across, span), f32(blocks * chunk, depth)),
        mid,
        pressure,
        courant,
        nonlinearity,
        absorption,
        own_map.T,
        slot_table.T,
        before,
        after,
        left,
        right,
        scratch_shapes=[scratch(deep, span), scratch(deep, span), scratch(span // 128, deep // 2 * across, 128)],
    )
    got = lax.all_to_all(send, ("gx", "gy"), split_axis=0, concat_axis=0, tiled=True)
    free, after_free = run(
        second_elastic,
        (f32(rows, cols, depth),) * 2,
        free,
        displacement,
        displacement_prev,
        layer_labels,
        shear_table,
        viscosity_table,
        before,
        after,
        left,
        right,
        scratch_shapes=[scratch(rows, depth)] * 4,
        tables=(4, 5),
    )
    tissue_force = run(functools.partial(land, capacity, chunk), f32(rows, cols, depth), got)
    up, down = swap(tissue_force[0], tissue_force[rows - 1], "gx")
    beside_l, beside_r = swap(tissue_force[:, 0], tissue_force[:, cols - 1], "gy")
    displacement_mid, displacement_new = run(
        last_steps,
        (f32(rows, cols, depth),) * 2,
        tissue_force,
        free,
        after_free,
        layer_labels,
        shear_table,
        viscosity_table,
        up,
        down,
        beside_l,
        beside_r,
        tables=(4, 5),
    )
    return (pressure_mid, pressure_new, tissue_force, displacement_mid, displacement_new)


def solution(mesh):
    block = P(("group", "gx"), "gy", None)
    plane = P(("group", "gx"), "gy")
    return jax.shard_map(
        local,
        mesh=mesh,
        in_specs=(block,) * 5 + (plane,) * 2 + (block,) * 3 + (P("group"),) * 2,
        out_specs=(block,) * 5,
        check_vma=False,
    )
```

```python
import functools

import jax
import jax.numpy as jnp
from jax import lax
from jax.experimental import pallas as pl
from jax.experimental.pallas import tpu as pltpu
from jax.sharding import PartitionSpec as P

VMEM = pl.BlockSpec(memory_space=pltpu.VMEM)
SMEM = pl.BlockSpec(memory_space=pltpu.SMEM)
EXACT = lax.Precision.HIGHEST


def lateral(x):
    dim, size = x.ndim - 1, x.shape[-1]
    lane = lax.broadcasted_iota(jnp.int32, x.shape, dim)
    lower = jnp.where(lane == 0, 0.0, pltpu.roll(x, 1, dim))
    upper = jnp.where(lane == size - 1, 0.0, pltpu.roll(x, size - 1, dim))
    return lower + upper


def beside(x, before, after):
    size = x.shape[0]
    row = lax.broadcasted_iota(jnp.int32, x.shape, 0)
    up = jnp.where(row == 0, before, pltpu.roll(x, 1, 0))
    down = jnp.where(row == size - 1, after, pltpu.roll(x, size - 1, 0))
    return up + down


def at_ends(shape, first, last):
    row = lax.broadcasted_iota(jnp.int32, shape, 0)
    return jnp.where(row == 0, first, jnp.where(row == shape[0] - 1, last, 0.0))


def wave(now, before, lap, courant, nonlinearity, absorption):
    return (
        2.0 * now
        - before
        + courant * lap
        + nonlinearity * (now * now - before * before)
        - 0.1 * absorption * (now - before)
    )


def lookup(kinds, table, first):
    result = jnp.zeros(kinds.shape, jnp.float32)
    for kind in range(table.shape[0]):
        result = jnp.where(kinds == kind + first, table[kind], result)
    return result


def halves(ref, base, x):
    half, depth = x.shape[0] // 2, x.shape[1]
    ref[base : base + half, 0:depth] = x[:half]
    ref[base : base + half, depth : 2 * depth] = x[half:]


def whole(ref, base, half, depth):
    return jnp.concatenate(
        [ref[base : base + half, 0:depth], ref[base : base + half, depth : 2 * depth]], axis=0
    )


def border_rows(*refs):
    fields, (shear, viscosity, first, last), buffers, sems = refs[:8], refs[8:12], refs[12:28], refs[28]
    copies = []
    for k, buffer in enumerate(buffers):
        field, count = fields[k // 2], buffer.shape[0]
        start = 0 if k % 2 == 0 else field.shape[0] - count
        copies.append(
            pltpu.make_async_copy(field.at[pl.ds(start, count)], buffer, sems.at[k])
        )
    for copy in copies:
        copy.start()
    for copy in copies:
        copy.wait()
    p0, p1, q0, q1, c0, c1, n0, n1, a0, a1, d0, d1, e0, e1, l0, l1 = buffers
    sides = (
        (p0, 0, 1, q0, c0, n0, a0, d0, e0, l0, first),
        (p1, 1, 0, q1, c1, n1, a1, d1, e1, l1, last),
    )
    for p_ref, at, inner, q_ref, c_ref, n_ref, a_ref, d_ref, b_ref, l_ref, out in sides:
        p, c = p_ref[at], c_ref[0]
        across, half = p.shape[0], d_ref.shape[1] // 2
        lap = p_ref[inner] + beside(p, 0.0, 0.0) + lateral(p) - 6.0 * p
        out[0:across] = p
        out[across : 2 * across] = c
        out[2 * across : 3 * across] = wave(p, q_ref[0], lap, c, n_ref[0], a_ref[0])
        d = d_ref[at]
        e = d - b_ref[at]
        d_in = d_ref[inner]
        e_in = d_in - b_ref[inner]
        labels = l_ref[0]
        s, v = lookup(labels, shear, 0), lookup(labels, viscosity, 0)
        lap_d = d_in + beside(d, 0.0, 0.0) + lateral(d) - 6.0 * d
        lap_e = e_in + beside(e, 0.0, 0.0) + lateral(e) - 6.0 * e
        base = 3 * across
        halves(out, base, d)
        halves(out, base + half, e)
        halves(out, base + 2 * half, d + e + s * lap_d + v * lap_e)
        halves(out, base + 3 * half, labels.astype(jnp.float32) + 1.0)


def border_columns(
    p_ref, q_ref, c_ref, n_ref, a_ref, d_ref, b_ref, l_ref, shear, viscosity, before, after, left, right
):
    deep, across, _ = p_ref.shape
    rows, cols, depth = d_ref.shape
    half = cols // 2
    row = lambda ref, base, j: ref[base + j : base + j + 1, :]
    base = 3 * across

    def line(ref, offset, j):
        at, lane = (j, 0) if j < half else (j - half, depth)
        return ref[base + offset + at : base + offset + at + 1, lane : lane + depth]

    for j, inner, k, k_in, out in (
        (0, 1, 0, 1, left),
        (across - 1, across - 2, cols - 1, cols - 2, right),
    ):
        p, c = p_ref[:, j, :], c_ref[:, j, :]
        p_up, p_down = row(before, 0, j), row(after, 0, j)
        lap = beside(p, p_up, p_down) + p_ref[:, inner, :] + lateral(p) - 6.0 * p
        out[0:deep] = p
        out[deep : 2 * deep] = c
        out[2 * deep : 3 * deep] = wave(
            p, q_ref[:, j, :], lap, c, n_ref[:, j, :], a_ref[:, j, :]
        )
        d = d_ref[:, k, :]
        e = d - b_ref[:, k, :]
        d_in = d_ref[:, k_in, :]
        e_in = d_in - b_ref[:, k_in, :]
        labels = l_ref[:, k, :]
        s, v = lookup(labels, shear, 0), lookup(labels, viscosity, 0)
        d_up, d_down = line(before, 0, k), line(after, 0, k)
        e_up, e_down = line(before, half, k), line(after, half, k)
        lap_d = beside(d, d_up, d_down) + d_in + lateral(d) - 6.0 * d
        lap_e = beside(e, e_up, e_down) + e_in + lateral(e) - 6.0 * e
        top = 3 * deep
        out[top : top + 1] = p_up
        out[top + 1 : top + 2] = p_down
        out[top + 2 : top + 3, 0:depth] = d_up
        out[top + 2 : top + 3, depth : 2 * depth] = e_up
        out[top + 3 : top + 4, 0:depth] = d_down
        out[top + 3 : top + 4, depth : 2 * depth] = e_down
        out[top + 4 : top + 8] = jnp.zeros((4, p.shape[1]), jnp.float32)
        out[top + 8 : top + 8 + rows, 0:depth] = d
        out[top + 8 : top + 8 + rows, depth : 2 * depth] = e
        out[top + 8 + rows : top + 8 + 2 * rows, 0:depth] = labels.astype(jnp.float32) + 1.0
        out[top + 8 + rows : top + 8 + 2 * rows, depth : 2 * depth] = (
            d + e + s * lap_d + v * lap_e
        )


def first_steps(
    p_ref, q_ref, c_ref, n_ref, a_ref, d_ref, b_ref, l_ref, shear, viscosity, before, after, mid, free
):
    deep, across, _ = p_ref.shape
    rows, cols, depth = d_ref.shape
    half = cols // 2
    base = 3 * across

    def acoustic(i, p_up, p_down):
        p = p_ref[i]
        lap = p_up + p_down + beside(p, 0.0, 0.0) + lateral(p) - 6.0 * p
        mid[i] = wave(p, q_ref[i], lap, c_ref[i], n_ref[i], a_ref[i])

    acoustic(0, before[0:across], p_ref[1])
    acoustic(deep - 1, p_ref[deep - 2], after[0:across])

    def acoustic_body(i, carry):
        acoustic(i, p_ref[i - 1], p_ref[i + 1])
        return carry

    lax.fori_loop(1, deep - 1, acoustic_body, 0)

    def elastic(i, d_up, d_down, e_up, e_down):
        d = d_ref[i]
        e = d - b_ref[i]
        s, v = lookup(l_ref[i], shear, 0), lookup(l_ref[i], viscosity, 0)
        lap_d = d_up + d_down + beside(d, 0.0, 0.0) + lateral(d) - 6.0 * d
        lap_e = e_up + e_down + beside(e, 0.0, 0.0) + lateral(e) - 6.0 * e
        free[i] = d + e + s * lap_d + v * lap_e

    change = lambda i: d_ref[i] - b_ref[i]
    elastic(
        0, whole(before, base, half, depth), d_ref[1], whole(before, base + half, half, depth), change(1)
    )
    elastic(
        rows - 1,
        d_ref[rows - 2],
        whole(after, base, half, depth),
        change(rows - 2),
        whole(after, base + half, half, depth),
    )

    def elastic_body(i, carry):
        elastic(i, d_ref[i - 1], d_ref[i + 1], change(i - 1), change(i + 1))
        return carry

    lax.fori_loop(1, rows - 1, elastic_body, 0)


def dot(x, y, contract=((1,), (0,))):
    return lax.dot_general(
        x, y, (contract, ((), ())), precision=EXACT, preferred_element_type=jnp.float32
    )


def selected(x, y):
    high = y.astype(jnp.bfloat16)
    low = (y - high.astype(jnp.float32)).astype(jnp.bfloat16)
    x = x.astype(jnp.bfloat16)
    product = functools.partial(jnp.dot, preferred_element_type=jnp.float32)
    return product(x, high) + product(x, low)


def iota(shape, dim):
    return lax.broadcasted_iota(jnp.int32, shape, dim)


def address(grid, tile, room, chunk, own_ref, slot_ref, match, placed):
    (tiles_down, tiles_across), (rows, cols) = grid, tile
    blocks, cells = tiles_down * tiles_across, rows * cols
    wide, tall = own_ref.shape
    count = wide * tall
    parts = match.shape[1] // count

    spread = (iota((tall, count), 1) // wide == iota((tall, count), 0)).astype(jnp.float32)
    mine = iota((wide, count), 1) % wide == iota((wide, count), 0)
    spread_t = (iota((count, tall), 0) // wide == iota((count, tall), 1)).astype(jnp.float32)
    mine_t = iota((count, wide), 0) % wide == iota((count, wide), 1)

    def flat(ref):
        x = ref[...].astype(jnp.float32)
        along = jnp.sum(jnp.where(mine, dot(x, spread), 0.0), axis=0, keepdims=True)
        down = dot(spread_t, x, ((1,), (1,)))
        down = jnp.sum(jnp.where(mine_t, down, 0.0), axis=1, keepdims=True)
        return along.astype(jnp.int32), down.astype(jnp.int32)

    def entries(own, slot):
        r, c = slot // cols, slot % cols
        tile_r, tile_c = own // tiles_across, own % tiles_across
        focal = own < blocks
        nobody = jnp.full(own.shape, -1, jnp.int32)
        up = focal & (r == 0) & (tile_r > 0)
        down = focal & (r == rows - 1) & (tile_r < tiles_down - 1)
        left = focal & (c == 0) & (tile_c > 0)
        right = focal & (c == cols - 1) & (tile_c < tiles_across - 1)
        to = (
            jnp.where(focal, own, nobody),
            jnp.where(up, own - tiles_across, jnp.where(down, own + tiles_across, nobody)),
            jnp.where(left, own - 1, jnp.where(right, own + 1, nobody)),
        )
        place = (
            slot,
            cells + c + jnp.where(up, cols, 0),
            cells + 2 * cols + r + jnp.where(left, rows, 0),
        )
        return to, place

    (own_row, own_col), (slot_row, slot_col) = flat(own_ref), flat(slot_ref)
    to_row, place_row = entries(own_row, slot_row)
    to_col, _ = entries(own_col, slot_col)
    ones = lambda x: jnp.where(x, 1.0, 0.0)
    earlier = iota((count, count), 0) < iota((count, count), 1)
    used, ranks = jnp.zeros(own_row.shape, jnp.float32), []
    for k in range(3):
        rank = jnp.zeros(own_row.shape, jnp.float32)
        for other in range(k + 1):
            same = to_col[other] == to_row[k]
            same = same & earlier if other == k else same
            rank = rank + jnp.sum(ones(same), axis=0, keepdims=True)
        ranks.append(rank.astype(jnp.int32))
        used = jnp.maximum(used, jnp.where(to_row[k] >= 0, rank + 1.0, 0.0))
    full = jnp.where(jnp.max(used) > room, 1.0, 0.0)
    total = blocks * chunk
    at = iota((total, count), 0)
    fits = [(to >= 0) & (rank < room) for to, rank in zip(to_row, ranks)]
    base = [
        jnp.where(fit, to * chunk + rank, -total) for fit, to, rank in zip(fits, to_row, ranks)
    ]
    for part in range(parts):
        here = at - part * room
        match[:, part * count : part * count + count] = sum(ones(here == b) for b in base)
    lanes = (128, count)
    row, lane = iota((total, 128), 0), iota((total, 128), 1)
    result = jnp.where((row % chunk == chunk - 1) & (lane == room), full, 0.0)
    for fit, to, rank, place in zip(fits, to_row, ranks, place_row):
        target = ones(at == jnp.where(fit, to * chunk + chunk - 1, -1))
        value = jnp.where(iota(lanes, 0) == rank, place.astype(jnp.float32) + 1.0, 0.0)
        result = result + dot(target, value, ((1,), (1,)))
    placed[...] = result


def second_acoustic(
    mid_ref,
    p_ref,
    c_ref,
    n_ref,
    a_ref,
    match_ref,
    placed_ref,
    before,
    after,
    left,
    right,
    mid,
    new,
    send,
    first_col,
    last_col,
    pairs,
):
    deep, across, span = p_ref.shape
    mid[...] = mid_ref[...]
    for j, side, beyond in ((0, left, first_col), (across - 1, right, last_col)):
        mid[:, j, :] = mid_ref[:, j, :] + c_ref[:, j, :] * side[0:deep]
        beyond[...] = side[2 * deep : 3 * deep] + side[deep : 2 * deep] * p_ref[:, j, :]
    top = 3 * deep

    def row_beyond(side, edge, k):
        c = side[across : 2 * across]
        corners = at_ends(c.shape, left[top + k : top + k + 1], right[top + k : top + k + 1])
        return side[2 * across : 3 * across] + c * (p_ref[edge] + corners)

    def step(i, up, down):
        m, p, c, a = mid[i], p_ref[i], c_ref[i], a_ref[i]
        sides = beside(m, first_col[pl.ds(i, 1), :], last_col[pl.ds(i, 1), :])
        lap = up + down + sides + lateral(m) - 6.0 * m
        result = wave(m, p, lap, c, n_ref[i], a)
        new[i] = result
        return 0.1 * a * (m * m + result * result) * lax.rsqrt(c)

    def put(k, value):
        at = pl.ds(pl.multiple_of(k * across, across), across)
        for part in range(span // 128):
            pairs[part, at, :] = value[:, part * 128 : part * 128 + 128]

    put(0, step(0, row_beyond(before, 0, 0), mid[1]) + step(1, mid[0], mid[2]))
    put(
        deep // 2 - 1,
        step(deep - 2, mid[deep - 3], mid[deep - 1])
        + step(deep - 1, mid[deep - 2], row_beyond(after, deep - 1, 1)),
    )

    def body(k, carry):
        i = 2 * k
        put(k, step(i, mid[i - 1], mid[i + 1]) + step(i + 1, mid[i], mid[i + 2]))
        return carry

    lax.fori_loop(1, deep // 2 - 1, body, 0)
    count = deep // 2 * (across // 2)
    paired = jnp.concatenate(
        [
            pairs[part, pl.ds(0, count, stride=2), :] + pairs[part, pl.ds(1, count, stride=2), :]
            for part in range(span // 128)
        ],
        axis=1,
    )
    pairing = iota((256, 128), 0) // 2 == iota((256, 128), 1)
    pairing = pairing.astype(jnp.float32).astype(jnp.bfloat16)
    high = paired.astype(jnp.bfloat16)
    low = (paired - high.astype(jnp.float32)).astype(jnp.bfloat16)
    product = functools.partial(jnp.dot, preferred_element_type=jnp.float32)
    lines = 0.125 * jnp.concatenate(
        [
            product(high[:, at : at + 256], pairing) + product(low[:, at : at + 256], pairing)
            for at in range(0, span, 256)
        ],
        axis=1,
    )
    count, depth = lines.shape
    parts = [lines[:, at : at + 128] for at in range(0, depth, 128)]
    send[...] = selected(match_ref[...], jnp.concatenate(parts, axis=0)) + placed_ref[...]


def second_elastic(
    free_ref, d_ref, b_ref, l_ref, shear, viscosity, before, after, left, right, free, after_free,
    d_first, d_last, f_first, f_last
):
    rows, cols, depth = d_ref.shape
    half = cols // 2
    across = (before.shape[0] - 2 * cols) // 3
    base = 3 * across
    top = left.shape[0] - 2 * rows - 8
    free[...] = free_ref[...]
    for j, side, d_col, f_col in ((0, left, d_first, f_first), (cols - 1, right, d_last, f_last)):
        labels = l_ref[:, j, :]
        s, v = lookup(labels, shear, 0), lookup(labels, viscosity, 0)
        d_side = side[top + 8 : top + 8 + rows, 0:depth]
        e_side = side[top + 8 : top + 8 + rows, depth : 2 * depth]
        free[:, j, :] = free_ref[:, j, :] + s * d_side + v * e_side
        kinds = side[top + 8 + rows : top + 8 + 2 * rows, 0:depth]
        s, v = lookup(kinds, shear, 1.0), lookup(kinds, viscosity, 1.0)
        d = d_ref[:, j, :]
        d_col[...] = d_side
        f_col[...] = (
            side[top + 8 + rows : top + 8 + 2 * rows, depth : 2 * depth]
            + s * d
            + v * (d - b_ref[:, j, :])
        )

    def beyond(side, edge, k):
        part = lambda n: whole(side, base + n * half, half, depth)
        d, kinds = part(0), part(3)
        s, v = lookup(kinds, shear, 1.0), lookup(kinds, viscosity, 1.0)
        d_edge = d_ref[edge]
        corner = lambda ref, lane: ref[top + k : top + k + 1, lane : lane + depth]
        d_ends = at_ends(d.shape, corner(left, 0), corner(right, 0))
        e_ends = at_ends(d.shape, corner(left, depth), corner(right, depth))
        f = part(2) + s * (d_edge + d_ends) + v * (d_edge - b_ref[edge] + e_ends)
        return f, d

    def step(i, f_up, f_down, d_up, d_down):
        f, d = free[i], d_ref[i]
        s, v = lookup(l_ref[i], shear, 0), lookup(l_ref[i], viscosity, 0)
        at = lambda ref: ref[pl.ds(i, 1), :]
        lap_f = f_up + f_down + beside(f, at(f_first), at(f_last)) + lateral(f) - 6.0 * f
        lap_d = d_up + d_down + beside(d, at(d_first), at(d_last)) + lateral(d) - 6.0 * d
        after_free[i] = 2.0 * f - d + s * lap_f + v * (lap_f - lap_d)

    f_up, d_up = beyond(before, 0, 2)
    step(0, f_up, free[1], d_up, d_ref[1])
    f_down, d_down = beyond(after, rows - 1, 3)
    step(rows - 1, free[rows - 2], f_down, d_ref[rows - 2], d_down)

    def body(i, carry):
        step(i, free[i - 1], free[i + 1], d_ref[i - 1], d_ref[i + 1])
        return carry

    lax.fori_loop(1, rows - 1, body, 0)


def landed(room, chunk, cells, got_ref, rows_of):
    total = got_ref.shape[0]
    parts, slots, _ = rows_of.shape
    blocks = total // chunk
    places = got_ref[pl.ds(chunk - 1, blocks, stride=chunk), :]
    for source in range(blocks):
        for part in range(parts):
            start = source * chunk + part * room
            rows_of[part, source * room : source * room + room, :] = got_ref[start : start + room, :]
    pick = jnp.where(iota((blocks, slots), 1) // room == iota((blocks, slots), 0), 1.0, 0.0)
    lanes = dot(places, pick, ((0,), (0,)))
    mine = iota(lanes.shape, 1) % room == iota(lanes.shape, 0)
    place = jnp.sum(jnp.where(mine, lanes, 0.0), axis=0, keepdims=True).astype(jnp.int32)
    landing = jnp.where(iota((cells, slots), 0) + 1 == place, 1.0, 0.0)
    return [selected(landing, rows_of[part]) for part in range(parts)]


def land(room, chunk, got_ref, force, rows_of):
    rows, cols, _ = force.shape
    for part, x in enumerate(landed(room, chunk, rows * cols, got_ref, rows_of)):
        force[:, :, part * 128 : part * 128 + 128] = x.reshape(rows, cols, 128)


def tissue_steps(force, free, after_free, l_ref, shear, viscosity, up, down, left, right, mid, new):
    rows = force.shape[0]

    def step(i, f_up, f_down):
        f = force[i]
        s, v = lookup(l_ref[i], shear, 0), lookup(l_ref[i], viscosity, 0)
        at = lambda ref: ref[pl.ds(i, 1), :]
        lap = f_up + f_down + beside(f, at(left), at(right)) + lateral(f) - 6.0 * f
        mid[i] = free[i] + 0.25 * f
        new[i] = after_free[i] + 0.75 * f + 0.25 * (s + v) * lap

    step(0, up[...], force[1])
    step(rows - 1, force[rows - 2], down[...])

    def body(i, carry):
        step(i, force[i - 1], force[i + 1])
        return carry

    lax.fori_loop(1, rows - 1, body, 0)


def land_and_step(
    room, chunk, got_ref, free, after_free, l_ref, shear, viscosity, force, mid, new,
    rows_of, up, down, left, right
):
    rows, cols, _ = force.shape
    cells = rows * cols
    borders, start = [], cells
    for ref in (up, down, left, right):
        borders.append((ref, start))
        start += ref.shape[0]
    for part, x in enumerate(landed(room, chunk, start, got_ref, rows_of)):
        lanes = slice(part * 128, part * 128 + 128)
        force[:, :, lanes] = x[:cells].reshape(rows, cols, 128)
        for ref, first in borders:
            ref[:, lanes] = x[first : first + ref.shape[0]]
    tissue_steps(
        force, free, after_free, l_ref, shear, viscosity, up, down, left, right, mid, new
    )


def swap(first, last, axis):
    size = lax.axis_size(axis)
    up = [(i, i + 1) for i in range(size - 1)]
    down = [(j, i) for i, j in up]
    return lax.ppermute(last, axis, up), lax.ppermute(first, axis, down)


def local(
    pressure,
    pressure_prev,
    courant,
    nonlinearity,
    absorption,
    own_map,
    slot_table,
    displacement,
    displacement_prev,
    layer_labels,
    shear_table,
    viscosity_table,
):
    deep, across, span = pressure.shape
    rows, cols, depth = displacement.shape
    f32 = lambda *shape: jax.ShapeDtypeStruct(shape, jnp.float32)
    params = pltpu.CompilerParams(vmem_limit_bytes=8 << 20)
    scratch = lambda *shape: pltpu.VMEM(shape, jnp.float32)

    def run(kernel, out, *args, scratch_shapes=(), tables=()):
        specs = [SMEM if k in tables else VMEM for k in range(len(args))]
        moved = 4 * sum(x.size for x in args) + 4 * sum(x.size for x in jax.tree.leaves(out))
        cost = pl.CostEstimate(flops=20 * moved, bytes_accessed=moved, transcendentals=0)
        return pl.pallas_call(
            kernel,
            out_shape=out,
            in_specs=specs,
            out_specs=jax.tree.map(lambda _: VMEM, out),
            scratch_shapes=scratch_shapes,
            compiler_params=params,
            cost_estimate=cost,
        )(*args)

    fields = (
        (pressure, 2),
        (pressure_prev, 1),
        (courant, 1),
        (nonlinearity, 1),
        (absorption, 1),
        (displacement, 2),
        (displacement_prev, 2),
        (layer_labels, 1),
    )
    face = 3 * across + 2 * cols
    first, last = pl.pallas_call(
        border_rows,
        out_shape=(f32(face, span), f32(face, span)),
        in_specs=[pl.BlockSpec(memory_space=pltpu.HBM)] * len(fields) + [SMEM, SMEM],
        out_specs=(VMEM, VMEM),
        scratch_shapes=[
            pltpu.VMEM((count,) + x.shape[1:], x.dtype) for x, count in fields for _ in range(2)
        ]
        + [pltpu.SemaphoreType.DMA((2 * len(fields),))],
        compiler_params=pltpu.CompilerParams(vmem_limit_bytes=55 << 20),
    )(*[x for x, _ in fields], shear_table, viscosity_table)
    before, after = swap(first, last, "gx")
    grid = (lax.axis_size("gx"), lax.axis_size("gy"))
    blocks = grid[0] * grid[1]
    capacity = max(2, deep // 2 * (across // 2) // blocks)
    parts = depth // 128
    room = 2 * capacity + 1
    chunk = -(-(room * parts + 1) // 8) * 8
    count = own_map.size
    match, placed = run(
        functools.partial(address, grid, (rows, cols), room, chunk),
        (f32(blocks * chunk, parts * count), f32(blocks * chunk, 128)),
        own_map.T,
        slot_table.T,
    )
    inputs = tuple(x for x, _ in fields) + (shear_table, viscosity_table, before, after)
    side = 3 * deep + 8 + 2 * rows
    first, last = run(border_columns, (f32(side, span),) * 2, *inputs, tables=(8, 9))
    left, right = swap(first, last, "gy")
    mid, free = run(
        first_steps, (f32(deep, across, span), f32(rows, cols, depth)), *inputs, tables=(8, 9)
    )
    pressure_mid, pressure_new, send = run(
        second_acoustic,
        (f32(deep, across, span), f32(deep, across, span), f32(blocks * chunk, 128)),
        mid,
        pressure,
        courant,
        nonlinearity,
        absorption,
        match,
        placed,
        before,
        after,
        left,
        right,
        scratch_shapes=[
            scratch(deep, span),
            scratch(deep, span),
            scratch(span // 128, deep // 2 * across, 128),
        ],
    )
    send = send.reshape(blocks, chunk, 128)
    got = lax.all_to_all(send, ("gx", "gy"), split_axis=0, concat_axis=0, tiled=True)
    free, after_free = run(
        second_elastic,
        (f32(rows, cols, depth),) * 2,
        free,
        displacement,
        displacement_prev,
        layer_labels,
        shear_table,
        viscosity_table,
        before,
        after,
        left,
        right,
        scratch_shapes=[scratch(rows, depth)] * 4,
        tables=(4, 5),
    )
    whole_block = f32(rows, cols, depth)
    arrived = scratch(depth // 128, blocks * room, 128)

    def direct(got, *rest):
        return run(
            functools.partial(land_and_step, room, chunk),
            (whole_block,) * 3,
            got,
            *rest,
            scratch_shapes=[arrived] + [scratch(n, depth) for n in (cols, cols, rows, rows)],
            tables=(4, 5),
        )

    def by_faces(got, *rest):
        force = run(
            functools.partial(land, room, chunk), whole_block, got, scratch_shapes=[arrived]
        )
        up, down = swap(force[0], force[rows - 1], "gx")
        at_left, at_right = swap(force[:, 0], force[:, cols - 1], "gy")
        mid, new = run(
            tissue_steps,
            (whole_block,) * 2,
            force,
            *rest,
            up,
            down,
            at_left,
            at_right,
            tables=(4, 5),
        )
        return force, mid, new

    tissue_force, displacement_mid, displacement_new = lax.cond(
        jnp.max(got[:, chunk - 1, room]) > 0.0,
        by_faces,
        direct,
        got.reshape(blocks * chunk, 128),
        free,
        after_free,
        layer_labels,
        shear_table,
        viscosity_table,
    )
    return (pressure_mid, pressure_new, tissue_force, displacement_mid, displacement_new)


def solution(mesh):
    block = P(("group", "gx"), "gy", None)
    plane = P(("group", "gx"), "gy")
    return jax.shard_map(
        local,
        mesh=mesh,
        in_specs=(block,) * 5 + (plane,) * 2 + (block,) * 3 + (P("group"),) * 2,
        out_specs=(block,) * 5,
        check_vma=False,
    )
```

```python
import functools
import math

import jax
import jax.numpy as jnp
from jax import lax
from jax.experimental import pallas as pl
from jax.experimental.pallas import tpu as pltpu
from jax.sharding import PartitionSpec as P

VMEM = pl.BlockSpec(memory_space=pltpu.VMEM)
SMEM = pl.BlockSpec(memory_space=pltpu.SMEM)
EXACT = lax.Precision.HIGHEST


def lateral(x):
    dim, size = x.ndim - 1, x.shape[-1]
    lane = lax.broadcasted_iota(jnp.int32, x.shape, dim)
    lower = jnp.where(lane == 0, 0.0, pltpu.roll(x, 1, dim))
    upper = jnp.where(lane == size - 1, 0.0, pltpu.roll(x, size - 1, dim))
    return lower + upper


def beside(x, before, after):
    size = x.shape[0]
    row = lax.broadcasted_iota(jnp.int32, x.shape, 0)
    up = jnp.where(row == 0, before, pltpu.roll(x, 1, 0))
    down = jnp.where(row == size - 1, after, pltpu.roll(x, size - 1, 0))
    return up + down


def at_ends(shape, first, last):
    row = lax.broadcasted_iota(jnp.int32, shape, 0)
    return jnp.where(row == 0, first, jnp.where(row == shape[0] - 1, last, 0.0))


def wave(now, before, lap, courant, nonlinearity, absorption):
    return (
        2.0 * now
        - before
        + courant * lap
        + nonlinearity * (now * now - before * before)
        - 0.1 * absorption * (now - before)
    )


def lookup(kinds, table, first):
    result = jnp.zeros(kinds.shape, jnp.float32)
    for kind in range(table.shape[0]):
        result = jnp.where(kinds == kind + first, table[kind], result)
    return result


def halves(ref, base, x):
    half, depth = x.shape[0] // 2, x.shape[1]
    ref[base : base + half, 0:depth] = x[:half]
    ref[base : base + half, depth : 2 * depth] = x[half:]


def whole(ref, base, half, depth):
    return jnp.concatenate(
        [ref[base : base + half, 0:depth], ref[base : base + half, depth : 2 * depth]], axis=0
    )


def border_columns(inner, *refs):
    count = len(inner)
    fields, (shear, viscosity, left, right) = refs[:count], refs[count : count + 4]
    buffers, sems = refs[count + 4 : -1], refs[-1]
    copies, sides, k = [], ([], []), 0
    for field, more in zip(fields, inner):
        last = field.shape[1] - 1
        for side, js in enumerate(((0, 1)[: 1 + more], (last, last - 1)[: 1 + more])):
            for j in js:
                copies.append(pltpu.make_async_copy(field.at[:, j, :], buffers[k], sems.at[k]))
                sides[side].append(buffers[k])
                k += 1
    for copy in copies:
        copy.start()
    for copy in copies:
        copy.wait()
    for columns, out in zip(sides, (left, right)):
        p, p_in, q, c, n, a, d, d_in, b, b_in, labels = [column[...] for column in columns]
        deep, (rows, depth) = p.shape[0], d.shape
        lap = beside(p, 0.0, 0.0) + p_in + lateral(p) - 6.0 * p
        out[0:deep] = p
        out[deep : 2 * deep] = c
        out[2 * deep : 3 * deep] = wave(p, q, lap, c, n, a)
        e, e_in = d - b, d_in - b_in
        s, v = lookup(labels, shear, 0), lookup(labels, viscosity, 0)
        lap_d = beside(d, 0.0, 0.0) + d_in + lateral(d) - 6.0 * d
        lap_e = beside(e, 0.0, 0.0) + e_in + lateral(e) - 6.0 * e
        top = 3 * deep
        first, last = slice(0, depth), slice(depth, 2 * depth)
        out[top : top + rows, first] = d
        out[top : top + rows, last] = e
        out[top + rows : top + 2 * rows, first] = labels.astype(jnp.float32) + 1.0
        out[top + rows : top + 2 * rows, last] = d + e + s * lap_d + v * lap_e


def cover(_, out):
    out[...] = jnp.zeros_like(out)


def first_steps(p_ref, q_ref, c_ref, n_ref, a_ref, d_ref, b_ref, l_ref, shear, viscosity, _, mid, free):
    deep, rows = p_ref.shape[0], d_ref.shape[0]

    def acoustic(i, p_up, p_down):
        p = p_ref[i]
        lap = p_up + p_down + beside(p, 0.0, 0.0) + lateral(p) - 6.0 * p
        mid[i] = wave(p, q_ref[i], lap, c_ref[i], n_ref[i], a_ref[i])

    acoustic(0, 0.0, p_ref[1])
    acoustic(deep - 1, p_ref[deep - 2], 0.0)

    def acoustic_body(i, carry):
        acoustic(i, p_ref[i - 1], p_ref[i + 1])
        return carry

    lax.fori_loop(1, deep - 1, acoustic_body, 0)

    def elastic(i, d_up, d_down, e_up, e_down):
        d = d_ref[i]
        e = d - b_ref[i]
        s, v = lookup(l_ref[i], shear, 0), lookup(l_ref[i], viscosity, 0)
        lap_d = d_up + d_down + beside(d, 0.0, 0.0) + lateral(d) - 6.0 * d
        lap_e = e_up + e_down + beside(e, 0.0, 0.0) + lateral(e) - 6.0 * e
        free[i] = d + e + s * lap_d + v * lap_e

    change = lambda i: d_ref[i] - b_ref[i]
    elastic(0, 0.0, d_ref[1], 0.0, change(1))
    elastic(rows - 1, d_ref[rows - 2], 0.0, change(rows - 2), 0.0)

    def elastic_body(i, carry):
        elastic(i, d_ref[i - 1], d_ref[i + 1], change(i - 1), change(i + 1))
        return carry

    lax.fori_loop(1, rows - 1, elastic_body, 0)


def border_rows(
    p_ref, c_ref, mid_ref, d_ref, b_ref, l_ref, free_ref, shear, viscosity, left, right, up, down
):
    deep, across, _ = p_ref.shape
    rows, cols, depth = d_ref.shape
    half = cols // 2
    top, base, end = 3 * deep, 3 * across, 3 * across + 2 * cols
    first, last = slice(0, depth), slice(depth, 2 * depth)
    for i, k, out in ((0, 0, up), (deep - 1, rows - 1, down)):
        p, c = p_ref[i], c_ref[i]
        p_left, p_right = left[i : i + 1], right[i : i + 1]
        out[0:across] = p
        out[across : 2 * across] = c
        out[2 * across : 3 * across] = mid_ref[i] + c * at_ends(c.shape, p_left, p_right)
        d, labels = d_ref[k], l_ref[k]
        s, v = lookup(labels, shear, 0), lookup(labels, viscosity, 0)
        at = slice(top + k, top + k + 1)
        d_ends = at_ends(d.shape, left[at, first], right[at, first])
        e_ends = at_ends(d.shape, left[at, last], right[at, last])
        halves(out, base, d)
        halves(out, base + half, d - b_ref[k])
        halves(out, base + 2 * half, free_ref[k] + s * d_ends + v * e_ends)
        halves(out, base + 3 * half, labels.astype(jnp.float32) + 1.0)
        out[end : end + 1] = p_left
        out[end + 1 : end + 2] = p_right
        out[end + 2 : end + 3] = left[at]
        out[end + 3 : end + 4] = right[at]
        out[end + 4 : end + 8] = jnp.zeros((4, out.shape[1]), jnp.float32)


def dot(x, y, contract=((1,), (0,))):
    return lax.dot_general(
        x, y, (contract, ((), ())), precision=EXACT, preferred_element_type=jnp.float32
    )


def selected(x, y):
    high = y.astype(jnp.bfloat16)
    low = (y - high.astype(jnp.float32)).astype(jnp.bfloat16)
    x = x.astype(jnp.bfloat16)
    product = functools.partial(jnp.dot, preferred_element_type=jnp.float32)
    return product(x, high) + product(x, low)


def iota(shape, dim):
    return lax.broadcasted_iota(jnp.int32, shape, dim)


def address(grid, tile, room, chunk, own_ref, slot_ref, _, match, placed):
    (tiles_down, tiles_across), (rows, cols) = grid, tile
    blocks, cells = tiles_down * tiles_across, rows * cols
    wide, tall = own_ref.shape
    count = wide * tall
    parts = match.shape[1] // count

    spread = (iota((tall, count), 1) // wide == iota((tall, count), 0)).astype(jnp.float32)
    mine = iota((wide, count), 1) % wide == iota((wide, count), 0)
    spread_t = (iota((count, tall), 0) // wide == iota((count, tall), 1)).astype(jnp.float32)
    mine_t = iota((count, wide), 0) % wide == iota((count, wide), 1)

    def flat(ref):
        x = ref[...].astype(jnp.float32)
        along = jnp.sum(jnp.where(mine, dot(x, spread), 0.0), axis=0, keepdims=True)
        down = dot(spread_t, x, ((1,), (1,)))
        down = jnp.sum(jnp.where(mine_t, down, 0.0), axis=1, keepdims=True)
        return along.astype(jnp.int32), down.astype(jnp.int32)

    def entries(own, slot):
        r, c = slot // cols, slot % cols
        tile_r, tile_c = own // tiles_across, own % tiles_across
        focal = own < blocks
        nobody = jnp.full(own.shape, -1, jnp.int32)
        up = focal & (r == 0) & (tile_r > 0)
        down = focal & (r == rows - 1) & (tile_r < tiles_down - 1)
        left = focal & (c == 0) & (tile_c > 0)
        right = focal & (c == cols - 1) & (tile_c < tiles_across - 1)
        to = (
            jnp.where(focal, own, nobody),
            jnp.where(up, own - tiles_across, jnp.where(down, own + tiles_across, nobody)),
            jnp.where(left, own - 1, jnp.where(right, own + 1, nobody)),
        )
        place = (
            slot,
            cells + c + jnp.where(up, cols, 0),
            cells + 2 * cols + r + jnp.where(left, rows, 0),
        )
        return to, place

    (own_row, own_col), (slot_row, slot_col) = flat(own_ref), flat(slot_ref)
    to_row, place_row = entries(own_row, slot_row)
    to_col, _ = entries(own_col, slot_col)
    ones = lambda x: jnp.where(x, 1.0, 0.0)
    earlier = iota((count, count), 0) < iota((count, count), 1)
    used, ranks = jnp.zeros(own_row.shape, jnp.float32), []
    for k in range(3):
        rank = jnp.zeros(own_row.shape, jnp.float32)
        for other in range(k + 1):
            same = to_col[other] == to_row[k]
            same = same & earlier if other == k else same
            rank = rank + jnp.sum(ones(same), axis=0, keepdims=True)
        ranks.append(rank.astype(jnp.int32))
        used = jnp.maximum(used, jnp.where(to_row[k] >= 0, rank + 1.0, 0.0))
    full = jnp.where(jnp.max(used) > room, 1.0, 0.0)
    total = blocks * chunk
    at = iota((total, count), 0)
    fits = [(to >= 0) & (rank < room) for to, rank in zip(to_row, ranks)]
    base = [
        jnp.where(fit, to * chunk + rank, -total) for fit, to, rank in zip(fits, to_row, ranks)
    ]
    for part in range(parts):
        here = at - part * room
        match[:, part * count : part * count + count] = sum(ones(here == b) for b in base)
    lanes = (128, count)
    row, lane = iota((total, 128), 0), iota((total, 128), 1)
    result = jnp.where((row % chunk == chunk - 1) & (lane == room), full, 0.0)
    for fit, to, rank, place in zip(fits, to_row, ranks, place_row):
        target = ones(at == jnp.where(fit, to * chunk + chunk - 1, -1))
        value = jnp.where(iota(lanes, 0) == rank, place.astype(jnp.float32) + 1.0, 0.0)
        result = result + dot(target, value, ((1,), (1,)))
    placed[...] = result


def radiated(m, new, courant, absorption):
    return 0.1 * absorption * (m * m + new * new) * lax.rsqrt(courant)


def paired_lanes(x):
    pairing = iota((256, 128), 0) // 2 == iota((256, 128), 1)
    pairing = pairing.astype(jnp.float32).astype(jnp.bfloat16)
    high = x.astype(jnp.bfloat16)
    low = (x - high.astype(jnp.float32)).astype(jnp.bfloat16)
    product = functools.partial(jnp.dot, preferred_element_type=jnp.float32)
    return [
        product(high[:, at : at + 256], pairing) + product(low[:, at : at + 256], pairing)
        for at in range(0, x.shape[1], 256)
    ]


def even_and_odd(ref, count):
    return jnp.concatenate(
        [
            ref[part, pl.ds(0, count, stride=2), :] + ref[part, pl.ds(1, count, stride=2), :]
            for part in range(ref.shape[0])
        ],
        axis=1,
    )


def step_rows(i, m, up, down, first, last, p_ref, c_ref, n_ref, a_ref):
    c, a = c_ref[i], a_ref[i]
    lap = up + down + beside(m, first, last) + lateral(m) - 6.0 * m
    new = wave(m, p_ref[i], lap, c, n_ref[i], a)
    return new, radiated(m, new, c, a)


def put(ref, start, value):
    for part in range(ref.shape[0]):
        ref[part, pl.ds(start, value.shape[0]), :] = value[:, part * 128 : part * 128 + 128]


def second_acoustic(
    p_ref, c_ref, n_ref, a_ref, mid_ref, left, right, mid, new, lines, beyond_l, beyond_r, pairs
):
    deep, across, _ = p_ref.shape
    mid[...] = mid_ref[...]
    for j, side, beyond in ((0, left, beyond_l), (across - 1, right, beyond_r)):
        mid[:, j, :] = mid_ref[:, j, :] + c_ref[:, j, :] * side[0:deep]
        beyond[...] = side[2 * deep : 3 * deep] + side[deep : 2 * deep] * p_ref[:, j, :]

    def body(k, carry):
        i = 2 * k
        total = 0.0
        for at in (i, i + 1):
            one = pl.ds(at, 1)
            result, force = step_rows(
                at, mid[at], mid[at - 1], mid[at + 1], beyond_l[one, :], beyond_r[one, :],
                p_ref, c_ref, n_ref, a_ref,
            )
            new[at] = result
            total = total + force
        put(pairs, pl.multiple_of(k * across, across), total)
        return carry

    for at in (0, 1, deep - 2, deep - 1):
        new[at] = jnp.zeros(new.shape[1:], jnp.float32)
    put(pairs, 0, jnp.zeros(new.shape[1:], jnp.float32))
    put(pairs, (deep // 2 - 1) * across, jnp.zeros(new.shape[1:], jnp.float32))
    lax.fori_loop(1, deep // 2 - 1, body, 0)
    count = deep // 2 * (across // 2)
    for part, x in enumerate(paired_lanes(even_and_odd(pairs, count))):
        lines[part * count : part * count + count] = 0.125 * x


def ends_and_send(
    p_ref, c_ref, n_ref, a_ref, mid_ref, lines_ref, match_ref, placed_ref,
    before, after, left, right, mids, news, send, lines, pairs
):
    deep, across, _ = p_ref.shape
    count = deep // 2 * (across // 2)
    cols = (before.shape[0] - 8 - 3 * across) // 2
    corners = 3 * across + 2 * cols
    lines[...] = lines_ref[...]
    media = (p_ref, c_ref, n_ref, a_ref)

    def beyond(side, j, i):
        return side[2 * deep + i : 2 * deep + i + 1] + side[deep + i : deep + i + 1] * p_ref[
            i, j : j + 1, :
        ]

    for k, (i, inner, more, side) in enumerate(
        ((0, 1, 2, before), (deep - 1, deep - 2, deep - 3, after))
    ):
        m = mid_ref[i] + c_ref[i] * side[0:across]
        m_in = mid_ref[inner]
        outer = side[2 * across : 3 * across] + side[across : 2 * across] * p_ref[i]
        first = beyond(left, 0, i) + left[deep + i : deep + i + 1] * side[corners : corners + 1]
        last = (
            beyond(right, across - 1, i)
            + right[deep + i : deep + i + 1] * side[corners + 1 : corners + 2]
        )
        new, force = step_rows(i, m, outer, m_in, first, last, *media)
        first, last = beyond(left, 0, inner), beyond(right, across - 1, inner)
        new_in, force_in = step_rows(inner, m_in, m, mid_ref[more], first, last, *media)
        mids[k] = m
        news[2 * k] = new
        news[2 * k + 1] = new_in
        put(pairs, 0, force + force_in)
        half = across // 2
        for part, x in enumerate(paired_lanes(even_and_odd(pairs, half))):
            at = part * count + (0 if k == 0 else count - half)
            lines[at : at + half] = 0.125 * x
    send[...] = selected(match_ref[...], lines[...]) + placed_ref[...]


def second_elastic(
    mid_ref, new_ref, mids, news, free_ref, d_ref, b_ref, l_ref, shear, viscosity,
    before, after, left, right, mid, new, free, after_free, d_first, d_last, f_first, f_last
):
    deep, across, _ = mid.shape
    mid[...] = mid_ref[...]
    new[...] = new_ref[...]
    for k, (i, inner) in enumerate(((0, 1), (deep - 1, deep - 2))):
        mid[i] = mids[k]
        new[i] = news[2 * k]
        new[inner] = news[2 * k + 1]
    rows, cols, depth = d_ref.shape
    half = cols // 2
    top, base, corners = 3 * deep, 3 * across, 3 * across + 2 * cols
    lanes, others = slice(0, depth), slice(depth, 2 * depth)
    free[...] = free_ref[...]
    for i, side in ((0, before), (rows - 1, after)):
        s, v = lookup(l_ref[i], shear, 0), lookup(l_ref[i], viscosity, 0)
        free[i] = (
            free_ref[i]
            + s * whole(side, base, half, depth)
            + v * whole(side, base + half, half, depth)
        )
    now, then = slice(top, top + rows), slice(top + rows, top + 2 * rows)
    for k, (j, side, d_col, f_col) in enumerate(
        ((0, left, d_first, f_first), (cols - 1, right, d_last, f_last))
    ):
        labels = l_ref[:, j, :]
        s, v = lookup(labels, shear, 0), lookup(labels, viscosity, 0)
        d_side, e_side = side[now, lanes], side[now, others]
        free[:, j, :] = free[:, j, :] + s * d_side + v * e_side
        kinds = side[then, lanes]
        s, v = lookup(kinds, shear, 1.0), lookup(kinds, viscosity, 1.0)
        d = d_ref[:, j, :]
        at = slice(corners + 2 + k, corners + 3 + k)
        d_ends = at_ends(d.shape, before[at, lanes], after[at, lanes])
        e_ends = at_ends(d.shape, before[at, others], after[at, others])
        d_col[...] = d_side
        f_col[...] = side[then, others] + s * (d + d_ends) + v * (d - b_ref[:, j, :] + e_ends)

    def beyond(side, edge):
        part = lambda n: whole(side, base + n * half, half, depth)
        d, kinds = part(0), part(3)
        s, v = lookup(kinds, shear, 1.0), lookup(kinds, viscosity, 1.0)
        d_edge = d_ref[edge]
        return part(2) + s * d_edge + v * (d_edge - b_ref[edge]), d

    def step(i, f_up, f_down, d_up, d_down):
        f, d = free[i], d_ref[i]
        s, v = lookup(l_ref[i], shear, 0), lookup(l_ref[i], viscosity, 0)
        at = lambda ref: ref[pl.ds(i, 1), :]
        lap_f = f_up + f_down + beside(f, at(f_first), at(f_last)) + lateral(f) - 6.0 * f
        lap_d = d_up + d_down + beside(d, at(d_first), at(d_last)) + lateral(d) - 6.0 * d
        after_free[i] = 2.0 * f - d + s * lap_f + v * (lap_f - lap_d)

    f_up, d_up = beyond(before, 0)
    step(0, f_up, free[1], d_up, d_ref[1])
    f_down, d_down = beyond(after, rows - 1)
    step(rows - 1, free[rows - 2], f_down, d_ref[rows - 2], d_down)

    def body(i, carry):
        step(i, free[i - 1], free[i + 1], d_ref[i - 1], d_ref[i + 1])
        return carry

    lax.fori_loop(1, rows - 1, body, 0)


def landed(room, chunk, cells, got_ref, rows_of):
    total = got_ref.shape[0]
    parts, slots, _ = rows_of.shape
    blocks = total // chunk
    places = got_ref[pl.ds(chunk - 1, blocks, stride=chunk), :]
    for source in range(blocks):
        for part in range(parts):
            start = source * chunk + part * room
            rows_of[part, source * room : source * room + room, :] = got_ref[start : start + room, :]
    pick = jnp.where(iota((blocks, slots), 1) // room == iota((blocks, slots), 0), 1.0, 0.0)
    lanes = dot(places, pick, ((0,), (0,)))
    mine = iota(lanes.shape, 1) % room == iota(lanes.shape, 0)
    place = jnp.sum(jnp.where(mine, lanes, 0.0), axis=0, keepdims=True).astype(jnp.int32)
    landing = jnp.where(iota((cells, slots), 0) + 1 == place, 1.0, 0.0)
    return [selected(landing, rows_of[part]) for part in range(parts)]


def land(room, chunk, got_ref, force, rows_of):
    rows, cols, _ = force.shape
    for part, x in enumerate(landed(room, chunk, rows * cols, got_ref, rows_of)):
        force[:, :, part * 128 : part * 128 + 128] = x.reshape(rows, cols, 128)


def tissue_steps(force, free, after_free, l_ref, shear, viscosity, up, down, left, right, mid, new):
    rows = force.shape[0]

    def step(i, f_up, f_down):
        f = force[i]
        s, v = lookup(l_ref[i], shear, 0), lookup(l_ref[i], viscosity, 0)
        at = lambda ref: ref[pl.ds(i, 1), :]
        lap = f_up + f_down + beside(f, at(left), at(right)) + lateral(f) - 6.0 * f
        mid[i] = free[i] + 0.25 * f
        new[i] = after_free[i] + 0.75 * f + 0.25 * (s + v) * lap

    step(0, up[...], force[1])
    step(rows - 1, force[rows - 2], down[...])

    def body(i, carry):
        step(i, force[i - 1], force[i + 1])
        return carry

    lax.fori_loop(1, rows - 1, body, 0)


def land_and_step(
    room, chunk, got_ref, free, after_free, l_ref, shear, viscosity, force, mid, new,
    rows_of, up, down, left, right
):
    rows, cols, _ = force.shape
    cells = rows * cols
    borders, start = [], cells
    for ref in (up, down, left, right):
        borders.append((ref, start))
        start += ref.shape[0]
    for part, x in enumerate(landed(room, chunk, start, got_ref, rows_of)):
        lanes = slice(part * 128, part * 128 + 128)
        force[:, :, lanes] = x[:cells].reshape(rows, cols, 128)
        for ref, first in borders:
            ref[:, lanes] = x[first : first + ref.shape[0]]
    tissue_steps(
        force, free, after_free, l_ref, shear, viscosity, up, down, left, right, mid, new
    )


def far(*arrays):
    return [pltpu.with_memory_space_constraint(x, pltpu.HBM) for x in arrays]


def swap(first, last, axis):
    size = lax.axis_size(axis)
    up = [(i, i + 1) for i in range(size - 1)]
    down = [(j, i) for i, j in up]
    return lax.ppermute(last, axis, up), lax.ppermute(first, axis, down)


def local(
    pressure,
    pressure_prev,
    courant,
    nonlinearity,
    absorption,
    own_map,
    slot_table,
    displacement,
    displacement_prev,
    layer_labels,
    shear_table,
    viscosity_table,
):
    deep, across, span = pressure.shape
    rows, cols, depth = displacement.shape
    f32 = lambda *shape: jax.ShapeDtypeStruct(shape, jnp.float32)
    hbm = lambda *shape: pltpu.HBM(shape, jnp.float32)
    scratch = lambda *shape: pltpu.VMEM(shape, jnp.float32)

    def run(kernel, out, *args, scratch_shapes=(), tables=(), weight=1, limit=8):
        specs = [SMEM if k in tables else VMEM for k in range(len(args))]
        moved = weight * 4 * sum(math.prod(x.shape) for x in args + tuple(jax.tree.leaves(out)))
        cost = pl.CostEstimate(flops=20 * moved, bytes_accessed=moved, transcendentals=0)
        return pl.pallas_call(
            kernel,
            out_shape=out,
            in_specs=specs,
            out_specs=jax.tree.map(lambda _: VMEM, out),
            scratch_shapes=scratch_shapes,
            compiler_params=pltpu.CompilerParams(vmem_limit_bytes=limit << 20),
            cost_estimate=cost,
        )(*args)

    fields = (
        (pressure, 1),
        (pressure_prev, 0),
        (courant, 0),
        (nonlinearity, 0),
        (absorption, 0),
        (displacement, 1),
        (displacement_prev, 1),
        (layer_labels, 0),
    )
    arrays, inner = [x for x, _ in fields], [more for _, more in fields]
    side = 3 * deep + 2 * rows
    buffers = [
        pltpu.VMEM((x.shape[0], x.shape[2]), x.dtype)
        for x, more in fields
        for _ in range(2 * (1 + more))
    ]
    near = pl.BlockSpec(memory_space=pltpu.HBM)
    first, last = pl.pallas_call(
        functools.partial(border_columns, inner),
        out_shape=(f32(side, span),) * 2,
        in_specs=[near] * len(fields) + [SMEM, SMEM],
        out_specs=(VMEM, VMEM),
        scratch_shapes=buffers + [pltpu.SemaphoreType.DMA((len(buffers),))],
        compiler_params=pltpu.CompilerParams(vmem_limit_bytes=63 << 20),
    )(*far(*arrays), shear_table, viscosity_table)
    left, right = swap(first, last, "gy")
    pause = pl.pallas_call(
        cover,
        out_shape=f32(8, 128),
        in_specs=[near],
        out_specs=VMEM,
        compiler_params=pltpu.CompilerParams(vmem_limit_bytes=1 << 20),
        cost_estimate=pl.CostEstimate(flops=2 * 10**10, bytes_accessed=10**9, transcendentals=0),
    )(*far(first))
    block, tissue = f32(deep, across, span), f32(rows, cols, depth)
    mid, free = run(
        first_steps,
        (block, tissue),
        *arrays,
        shear_table,
        viscosity_table,
        pause,
        tables=(8, 9),
    )
    first, last = run(
        border_rows,
        (f32(3 * across + 2 * cols + 8, span),) * 2,
        pressure,
        courant,
        mid,
        displacement,
        displacement_prev,
        layer_labels,
        free,
        shear_table,
        viscosity_table,
        left,
        right,
        tables=(7, 8),
    )
    before, after = swap(first, last, "gx")
    grid = (lax.axis_size("gx"), lax.axis_size("gy"))
    blocks = grid[0] * grid[1]
    capacity = max(2, deep // 2 * (across // 2) // blocks)
    parts = depth // 128
    room = 2 * capacity + 1
    chunk = -(-(room * parts + 1) // 8) * 8
    count = own_map.size
    match, placed = pl.pallas_call(
        functools.partial(address, grid, (rows, cols), room, chunk),
        out_shape=(f32(blocks * chunk, parts * count), f32(blocks * chunk, 128)),
        in_specs=[VMEM, VMEM, near],
        out_specs=(VMEM, VMEM),
        compiler_params=pltpu.CompilerParams(vmem_limit_bytes=16 << 20),
        cost_estimate=pl.CostEstimate(flops=10**8, bytes_accessed=10**7, transcendentals=0),
    )(own_map.T, slot_table.T, *far(first))
    media = (pressure, courant, nonlinearity, absorption)
    mid, new, lines = run(
        second_acoustic,
        (block, block, f32(parts * count, 128)),
        *media,
        mid,
        left,
        right,
        scratch_shapes=[
            scratch(deep, span),
            scratch(deep, span),
            scratch(span // 128, deep // 2 * across, 128),
        ],
    )
    mids, news, send = run(
        ends_and_send,
        (hbm(2, across, span), hbm(4, across, span), hbm(blocks * chunk, 128)),
        *media,
        mid,
        lines,
        match,
        placed,
        before,
        after,
        left,
        right,
        scratch_shapes=[scratch(parts * count, 128), scratch(span // 128, across, 128)],
    )
    send = send.reshape(blocks, chunk, 128)
    got = lax.all_to_all(send, ("gx", "gy"), split_axis=0, concat_axis=0, tiled=True)
    pressure_mid, pressure_new, free, after_free = run(
        second_elastic,
        (block, block, tissue, tissue),
        *far(mid, new, mids, news, free, displacement, displacement_prev, layer_labels),
        shear_table,
        viscosity_table,
        *far(before, after, left, right),
        scratch_shapes=[scratch(rows, depth)] * 4,
        tables=(8, 9),
        limit=24,
    )
    arrived = scratch(depth // 128, blocks * room, 128)

    def direct(got, *rest):
        return run(
            functools.partial(land_and_step, room, chunk),
            (tissue,) * 3,
            got,
            *rest,
            scratch_shapes=[arrived] + [scratch(n, depth) for n in (cols, cols, rows, rows)],
            tables=(4, 5),
        )

    def by_faces(got, *rest):
        force = run(
            functools.partial(land, room, chunk), tissue, got, scratch_shapes=[arrived]
        )
        up, down = swap(force[0], force[rows - 1], "gx")
        at_left, at_right = swap(force[:, 0], force[:, cols - 1], "gy")
        mid, new = run(
            tissue_steps,
            (tissue,) * 2,
            force,
            *rest,
            up,
            down,
            at_left,
            at_right,
            tables=(4, 5),
        )
        return force, mid, new

    tissue_force, displacement_mid, displacement_new = lax.cond(
        jnp.max(got[:, chunk - 1, room]) > 0.0,
        by_faces,
        direct,
        got.reshape(blocks * chunk, 128),
        free,
        after_free,
        layer_labels,
        shear_table,
        viscosity_table,
    )
    return (pressure_mid, pressure_new, tissue_force, displacement_mid, displacement_new)


def solution(mesh):
    block = P(("group", "gx"), "gy", None)
    plane = P(("group", "gx"), "gy")
    return jax.shard_map(
        local,
        mesh=mesh,
        in_specs=(block,) * 5 + (plane,) * 2 + (block,) * 3 + (P("group"),) * 2,
        out_specs=(block,) * 5,
        check_vma=False,
    )
```

```python
import functools
import math

import jax
import jax.numpy as jnp
from jax import lax
from jax.experimental import pallas as pl
from jax.experimental.pallas import tpu as pltpu
from jax.sharding import PartitionSpec as P

VMEM = pl.BlockSpec(memory_space=pltpu.VMEM)
SMEM = pl.BlockSpec(memory_space=pltpu.SMEM)
EXACT = lax.Precision.HIGHEST


def lateral(x):
    tiles = [x[:, at : at + 128] for at in range(0, x.shape[1], 128)]
    lane = lax.broadcasted_iota(jnp.int32, tiles[0].shape, 1)
    lower = [0.0] + [pltpu.roll(tile, 1, 1) for tile in tiles]
    upper = [pltpu.roll(tile, 127, 1) for tile in tiles] + [0.0]
    sums = [
        jnp.where(lane == 0, lower[k], lower[k + 1])
        + jnp.where(lane == 127, upper[k + 1], upper[k])
        for k in range(len(tiles))
    ]
    return jnp.concatenate(sums, axis=1)


def beside(x, before, after):
    tiles = [x[at : at + 8] for at in range(0, x.shape[0], 8)]
    row = lax.broadcasted_iota(jnp.int32, tiles[0].shape, 0)
    up = [before] + [pltpu.roll(tile, 1, 0) for tile in tiles]
    down = [pltpu.roll(tile, 7, 0) for tile in tiles] + [after]
    sums = [
        jnp.where(row == 0, up[k], up[k + 1]) + jnp.where(row == 7, down[k + 1], down[k])
        for k in range(len(tiles))
    ]
    return jnp.concatenate(sums, axis=0)


def at_ends(shape, first, last):
    row = lax.broadcasted_iota(jnp.int32, shape, 0)
    return jnp.where(row == 0, first, jnp.where(row == shape[0] - 1, last, 0.0))


def wave(now, before, lap, courant, nonlinearity, absorption):
    return (
        2.0 * now
        - before
        + courant * lap
        + nonlinearity * (now * now - before * before)
        - 0.1 * absorption * (now - before)
    )


def lookup(kinds, table, first):
    values = [table[kind] for kind in range(len(table) if isinstance(table, list) else table.shape[0])]
    result = jnp.full(kinds.shape, 0.0 if first else values[0], jnp.float32)
    for kind in range(0 if first else 1, len(values)):
        result = jnp.where(kinds == kind + first, values[kind], result)
    return result


def halves(ref, base, x):
    half, depth = x.shape[0] // 2, x.shape[1]
    ref[base : base + half, 0:depth] = x[:half]
    ref[base : base + half, depth : 2 * depth] = x[half:]


def whole(ref, base, half, depth):
    return jnp.concatenate(
        [ref[base : base + half, 0:depth], ref[base : base + half, depth : 2 * depth]], axis=0
    )


def border_columns(inner, *refs):
    count = len(inner)
    fields, (shear, viscosity, left, right) = refs[:count], refs[count : count + 4]
    buffers, sems = refs[count + 4 : -1], refs[-1]
    copies, sides, k = [], ([], []), 0
    for field, more in zip(fields, inner):
        last = field.shape[1] - 1
        for side, js in enumerate(((0, 1)[: 1 + more], (last, last - 1)[: 1 + more])):
            for j in js:
                copies.append(pltpu.make_async_copy(field.at[:, j, :], buffers[k], sems.at[k]))
                sides[side].append(buffers[k])
                k += 1
    for copy in copies:
        copy.start()
    for copy in copies:
        copy.wait()
    for columns, out in zip(sides, (left, right)):
        p, p_in, q, c, n, a, d, d_in, b, b_in, labels = [column[...] for column in columns]
        deep, (rows, depth) = p.shape[0], d.shape
        lap = beside(p, 0.0, 0.0) + p_in + lateral(p) - 6.0 * p
        out[0:deep] = p
        out[deep : 2 * deep] = c
        out[2 * deep : 3 * deep] = wave(p, q, lap, c, n, a)
        e, e_in = d - b, d_in - b_in
        s, v = lookup(labels, shear, 0), lookup(labels, viscosity, 0)
        lap_d = beside(d, 0.0, 0.0) + d_in + lateral(d) - 6.0 * d
        lap_e = beside(e, 0.0, 0.0) + e_in + lateral(e) - 6.0 * e
        top = 3 * deep
        first, last = slice(0, depth), slice(depth, 2 * depth)
        out[top : top + rows, first] = d
        out[top : top + rows, last] = e
        out[top + rows : top + 2 * rows, first] = labels.astype(jnp.float32) + 1.0
        out[top + rows : top + 2 * rows, last] = d + e + s * lap_d + v * lap_e


def cover(_, out):
    out[...] = jnp.zeros_like(out)


def first_steps(p_ref, q_ref, c_ref, n_ref, a_ref, d_ref, b_ref, l_ref, shear, viscosity, _, mid, free):
    deep, rows = p_ref.shape[0], d_ref.shape[0]

    def acoustic(i, p_up, p_down):
        p = p_ref[i]
        lap = p_up + p_down + beside(p, 0.0, 0.0) + lateral(p) - 6.0 * p
        mid[i] = wave(p, q_ref[i], lap, c_ref[i], n_ref[i], a_ref[i])

    acoustic(0, 0.0, p_ref[1])
    acoustic(deep - 1, p_ref[deep - 2], 0.0)

    def acoustic_body(i, carry):
        acoustic(i, p_ref[i - 1], p_ref[i + 1])
        return carry

    lax.fori_loop(1, deep - 1, acoustic_body, 0)

    def elastic(i, d_up, d_down, e_up, e_down):
        d = d_ref[i]
        e = d - b_ref[i]
        s, v = lookup(l_ref[i], shear, 0), lookup(l_ref[i], viscosity, 0)
        lap_d = d_up + d_down + beside(d, 0.0, 0.0) + lateral(d) - 6.0 * d
        lap_e = e_up + e_down + beside(e, 0.0, 0.0) + lateral(e) - 6.0 * e
        free[i] = d + e + s * lap_d + v * lap_e

    change = lambda i: d_ref[i] - b_ref[i]
    elastic(0, 0.0, d_ref[1], 0.0, change(1))
    elastic(rows - 1, d_ref[rows - 2], 0.0, change(rows - 2), 0.0)

    def elastic_body(i, carry):
        elastic(i, d_ref[i - 1], d_ref[i + 1], change(i - 1), change(i + 1))
        return carry

    lax.fori_loop(1, rows - 1, elastic_body, 0)


def border_rows(
    p_ref, c_ref, mid_ref, d_ref, b_ref, l_ref, free_ref, shear, viscosity, left, right, up, down
):
    deep, across, _ = p_ref.shape
    rows, cols, depth = d_ref.shape
    half = cols // 2
    top, base, end = 3 * deep, 3 * across, 3 * across + 2 * cols
    first, last = slice(0, depth), slice(depth, 2 * depth)
    for i, k, out in ((0, 0, up), (deep - 1, rows - 1, down)):
        p, c = p_ref[i], c_ref[i]
        p_left, p_right = left[i : i + 1], right[i : i + 1]
        out[0:across] = p
        out[across : 2 * across] = c
        out[2 * across : 3 * across] = mid_ref[i] + c * at_ends(c.shape, p_left, p_right)
        d, labels = d_ref[k], l_ref[k]
        s, v = lookup(labels, shear, 0), lookup(labels, viscosity, 0)
        at = slice(top + k, top + k + 1)
        d_ends = at_ends(d.shape, left[at, first], right[at, first])
        e_ends = at_ends(d.shape, left[at, last], right[at, last])
        halves(out, base, d)
        halves(out, base + half, d - b_ref[k])
        halves(out, base + 2 * half, free_ref[k] + s * d_ends + v * e_ends)
        halves(out, base + 3 * half, labels.astype(jnp.float32) + 1.0)
        out[end : end + 1] = p_left
        out[end + 1 : end + 2] = p_right
        out[end + 2 : end + 3] = left[at]
        out[end + 3 : end + 4] = right[at]
        out[end + 4 : end + 8] = jnp.zeros((4, out.shape[1]), jnp.float32)


def dot(x, y, contract=((1,), (0,))):
    return lax.dot_general(
        x, y, (contract, ((), ())), precision=EXACT, preferred_element_type=jnp.float32
    )


def selected(x, y):
    high = y.astype(jnp.bfloat16)
    low = (y - high.astype(jnp.float32)).astype(jnp.bfloat16)
    x = x.astype(jnp.bfloat16)
    product = functools.partial(jnp.dot, preferred_element_type=jnp.float32)
    return product(x, high) + product(x, low)


def iota(shape, dim):
    return lax.broadcasted_iota(jnp.int32, shape, dim)


def address(grid, tile, room, chunk, own_ref, slot_ref, _, match, placed):
    (tiles_down, tiles_across), (rows, cols) = grid, tile
    blocks, cells = tiles_down * tiles_across, rows * cols
    wide, tall = own_ref.shape
    count = wide * tall
    parts = match.shape[1] // count

    spread = (iota((tall, count), 1) // wide == iota((tall, count), 0)).astype(jnp.float32)
    mine = iota((wide, count), 1) % wide == iota((wide, count), 0)
    spread_t = (iota((count, tall), 0) // wide == iota((count, tall), 1)).astype(jnp.float32)
    mine_t = iota((count, wide), 0) % wide == iota((count, wide), 1)

    def flat(ref):
        x = ref[...].astype(jnp.float32)
        along = jnp.sum(jnp.where(mine, dot(x, spread), 0.0), axis=0, keepdims=True)
        down = dot(spread_t, x, ((1,), (1,)))
        down = jnp.sum(jnp.where(mine_t, down, 0.0), axis=1, keepdims=True)
        return along.astype(jnp.int32), down.astype(jnp.int32)

    def entries(own, slot):
        r, c = slot // cols, slot % cols
        tile_r, tile_c = own // tiles_across, own % tiles_across
        focal = own < blocks
        nobody = jnp.full(own.shape, -1, jnp.int32)
        up = focal & (r == 0) & (tile_r > 0)
        down = focal & (r == rows - 1) & (tile_r < tiles_down - 1)
        left = focal & (c == 0) & (tile_c > 0)
        right = focal & (c == cols - 1) & (tile_c < tiles_across - 1)
        to = (
            jnp.where(focal, own, nobody),
            jnp.where(up, own - tiles_across, jnp.where(down, own + tiles_across, nobody)),
            jnp.where(left, own - 1, jnp.where(right, own + 1, nobody)),
        )
        place = (
            slot,
            cells + c + jnp.where(up, cols, 0),
            cells + 2 * cols + r + jnp.where(left, rows, 0),
        )
        return to, place

    (own_row, own_col), (slot_row, slot_col) = flat(own_ref), flat(slot_ref)
    to_row, place_row = entries(own_row, slot_row)
    to_col, _ = entries(own_col, slot_col)
    ones = lambda x: jnp.where(x, 1.0, 0.0)
    earlier = iota((count, count), 0) < iota((count, count), 1)
    used, ranks = jnp.zeros(own_row.shape, jnp.float32), []
    for k in range(3):
        rank = jnp.zeros(own_row.shape, jnp.float32)
        for other in range(k + 1):
            same = to_col[other] == to_row[k]
            same = same & earlier if other == k else same
            rank = rank + jnp.sum(ones(same), axis=0, keepdims=True)
        ranks.append(rank.astype(jnp.int32))
        used = jnp.maximum(used, jnp.where(to_row[k] >= 0, rank + 1.0, 0.0))
    full = jnp.where(jnp.max(used) > room, 1.0, 0.0)
    total = blocks * chunk
    at = iota((total, count), 0)
    fits = [(to >= 0) & (rank < room) for to, rank in zip(to_row, ranks)]
    base = [
        jnp.where(fit, to * chunk + rank, -total) for fit, to, rank in zip(fits, to_row, ranks)
    ]
    for part in range(parts):
        here = at - part * room
        match[:, part * count : part * count + count] = sum(ones(here == b) for b in base)
    lanes = (128, count)
    row, lane = iota((total, 128), 0), iota((total, 128), 1)
    result = jnp.where((row % chunk == chunk - 1) & (lane == room), full, 0.0)
    for fit, to, rank, place in zip(fits, to_row, ranks, place_row):
        target = ones(at == jnp.where(fit, to * chunk + chunk - 1, -1))
        value = jnp.where(iota(lanes, 0) == rank, place.astype(jnp.float32) + 1.0, 0.0)
        result = result + dot(target, value, ((1,), (1,)))
    placed[...] = result


def radiated(m, new, courant, absorption):
    return 0.1 * absorption * (m * m + new * new) * lax.rsqrt(courant)


def paired_lanes(x):
    pairing = iota((256, 128), 0) // 2 == iota((256, 128), 1)
    pairing = pairing.astype(jnp.float32).astype(jnp.bfloat16)
    high = x.astype(jnp.bfloat16)
    low = (x - high.astype(jnp.float32)).astype(jnp.bfloat16)
    product = functools.partial(jnp.dot, preferred_element_type=jnp.float32)
    return [
        product(high[:, at : at + 256], pairing) + product(low[:, at : at + 256], pairing)
        for at in range(0, x.shape[1], 256)
    ]


def even_and_odd(ref, count):
    return jnp.concatenate(
        [
            ref[part, pl.ds(0, count, stride=2), :] + ref[part, pl.ds(1, count, stride=2), :]
            for part in range(ref.shape[0])
        ],
        axis=1,
    )


def step_rows(i, m, up, down, first, last, p_ref, c_ref, n_ref, a_ref):
    c, a = c_ref[i], a_ref[i]
    lap = up + down + beside(m, first, last) + lateral(m) - 6.0 * m
    new = wave(m, p_ref[i], lap, c, n_ref[i], a)
    return new, radiated(m, new, c, a)


def put(ref, start, value):
    for part in range(ref.shape[0]):
        ref[part, pl.ds(start, value.shape[0]), :] = value[:, part * 128 : part * 128 + 128]


def second_acoustic(
    p_ref, c_ref, n_ref, a_ref, mid_ref, left, right, mid, new, lines, beyond_l, beyond_r, pairs
):
    deep, across, _ = p_ref.shape
    mid[...] = mid_ref[...]
    for j, side, beyond in ((0, left, beyond_l), (across - 1, right, beyond_r)):
        mid[:, j, :] = mid_ref[:, j, :] + c_ref[:, j, :] * side[0:deep]
        beyond[...] = side[2 * deep : 3 * deep] + side[deep : 2 * deep] * p_ref[:, j, :]

    def body(k, carry):
        i = 2 * k
        total = 0.0
        for at in (i, i + 1):
            one = pl.ds(at, 1)
            result, force = step_rows(
                at, mid[at], mid[at - 1], mid[at + 1], beyond_l[one, :], beyond_r[one, :],
                p_ref, c_ref, n_ref, a_ref,
            )
            new[at] = result
            total = total + force
        put(pairs, pl.multiple_of(k * across, across), total)
        return carry

    for at in (0, 1, deep - 2, deep - 1):
        new[at] = jnp.zeros(new.shape[1:], jnp.float32)
    put(pairs, 0, jnp.zeros(new.shape[1:], jnp.float32))
    put(pairs, (deep // 2 - 1) * across, jnp.zeros(new.shape[1:], jnp.float32))
    lax.fori_loop(1, deep // 2 - 1, body, 0)
    count = deep // 2 * (across // 2)
    for part, x in enumerate(paired_lanes(even_and_odd(pairs, count))):
        lines[part * count : part * count + count] = 0.125 * x


def ends_and_send(
    p_ref, c_ref, n_ref, a_ref, mid_ref, lines_ref, match_ref, placed_ref,
    before, after, left, right, mids, news, send, lines, pairs
):
    deep, across, _ = p_ref.shape
    count = deep // 2 * (across // 2)
    cols = (before.shape[0] - 8 - 3 * across) // 2
    corners = 3 * across + 2 * cols
    lines[...] = lines_ref[...]
    media = (p_ref, c_ref, n_ref, a_ref)

    def beyond(side, j, i):
        return side[2 * deep + i : 2 * deep + i + 1] + side[deep + i : deep + i + 1] * p_ref[
            i, j : j + 1, :
        ]

    for k, (i, inner, more, side) in enumerate(
        ((0, 1, 2, before), (deep - 1, deep - 2, deep - 3, after))
    ):
        m = mid_ref[i] + c_ref[i] * side[0:across]
        m_in = mid_ref[inner]
        outer = side[2 * across : 3 * across] + side[across : 2 * across] * p_ref[i]
        first = beyond(left, 0, i) + left[deep + i : deep + i + 1] * side[corners : corners + 1]
        last = (
            beyond(right, across - 1, i)
            + right[deep + i : deep + i + 1] * side[corners + 1 : corners + 2]
        )
        new, force = step_rows(i, m, outer, m_in, first, last, *media)
        first, last = beyond(left, 0, inner), beyond(right, across - 1, inner)
        new_in, force_in = step_rows(inner, m_in, m, mid_ref[more], first, last, *media)
        mids[k] = m
        news[2 * k] = new
        news[2 * k + 1] = new_in
        put(pairs, 0, force + force_in)
        half = across // 2
        for part, x in enumerate(paired_lanes(even_and_odd(pairs, half))):
            at = part * count + (0 if k == 0 else count - half)
            lines[at : at + half] = 0.125 * x
    send[...] = selected(match_ref[...], lines[...]) + placed_ref[...]


def second_elastic(
    mid_ref, new_ref, mids, news, free_ref, d_ref, b_ref, l_ref, shear, viscosity,
    before, after, left, right, mid, new, free, after_free, quarter, d_first, d_last, f_first, f_last
):
    deep, across, _ = mid.shape
    mid[...] = mid_ref[...]
    new[...] = new_ref[...]
    for k, (i, inner) in enumerate(((0, 1), (deep - 1, deep - 2))):
        mid[i] = mids[k]
        new[i] = news[2 * k]
        new[inner] = news[2 * k + 1]
    rows, cols, depth = d_ref.shape
    half = cols // 2
    top, base, corners = 3 * deep, 3 * across, 3 * across + 2 * cols
    lanes, others = slice(0, depth), slice(depth, 2 * depth)
    free[...] = free_ref[...]
    for i, side in ((0, before), (rows - 1, after)):
        s, v = lookup(l_ref[i], shear, 0), lookup(l_ref[i], viscosity, 0)
        free[i] = (
            free_ref[i]
            + s * whole(side, base, half, depth)
            + v * whole(side, base + half, half, depth)
        )
    now, then = slice(top, top + rows), slice(top + rows, top + 2 * rows)
    for k, (j, side, d_col, f_col) in enumerate(
        ((0, left, d_first, f_first), (cols - 1, right, d_last, f_last))
    ):
        labels = l_ref[:, j, :]
        s, v = lookup(labels, shear, 0), lookup(labels, viscosity, 0)
        d_side, e_side = side[now, lanes], side[now, others]
        free[:, j, :] = free[:, j, :] + s * d_side + v * e_side
        kinds = side[then, lanes]
        s, v = lookup(kinds, shear, 1.0), lookup(kinds, viscosity, 1.0)
        d = d_ref[:, j, :]
        at = slice(corners + 2 + k, corners + 3 + k)
        d_ends = at_ends(d.shape, before[at, lanes], after[at, lanes])
        e_ends = at_ends(d.shape, before[at, others], after[at, others])
        d_col[...] = d_side
        f_col[...] = side[then, others] + s * (d + d_ends) + v * (d - b_ref[:, j, :] + e_ends)

    def beyond(side, edge):
        part = lambda n: whole(side, base + n * half, half, depth)
        d, kinds = part(0), part(3)
        s, v = lookup(kinds, shear, 1.0), lookup(kinds, viscosity, 1.0)
        d_edge = d_ref[edge]
        return part(2) + s * d_edge + v * (d_edge - b_ref[edge]), d

    def step(i, f_up, f_down, d_up, d_down):
        f, d = free[i], d_ref[i]
        s, v = lookup(l_ref[i], shear, 0), lookup(l_ref[i], viscosity, 0)
        at = lambda ref: ref[pl.ds(i, 1), :]
        lap_f = f_up + f_down + beside(f, at(f_first), at(f_last)) + lateral(f) - 6.0 * f
        lap_d = d_up + d_down + beside(d, at(d_first), at(d_last)) + lateral(d) - 6.0 * d
        after_free[i] = 2.0 * f - d + s * lap_f + v * (lap_f - lap_d)
        quarter[i] = 0.25 * (s + v)

    f_up, d_up = beyond(before, 0)
    step(0, f_up, free[1], d_up, d_ref[1])
    f_down, d_down = beyond(after, rows - 1)
    step(rows - 1, free[rows - 2], f_down, d_ref[rows - 2], d_down)

    def body(i, carry):
        step(i, free[i - 1], free[i + 1], d_ref[i - 1], d_ref[i + 1])
        return carry

    lax.fori_loop(1, rows - 1, body, 0)


def landed(room, chunk, cells, got_ref, rows_of):
    total = got_ref.shape[0]
    parts, slots, _ = rows_of.shape
    blocks = total // chunk
    slot = slots // blocks
    for source in range(blocks):
        for part in range(parts):
            start = source * chunk + part * room
            size = min(slot, total - start)
            at = source * slot
            rows_of[part, at : at + size, :] = got_ref[start : start + size, :]
            if size < slot:
                rows_of[part, at + size : at + slot, :] = jnp.zeros((slot - size, 128), jnp.float32)
    places, group = [], 128 // slot
    for first in range(0, blocks, group):
        x = got_ref[pl.ds(first * chunk + chunk - 1, group, stride=chunk), :]
        x = jnp.where(iota(x.shape, 1) < room, x, 0.0)
        x = pltpu.roll(x, 0, 1, stride=slot, stride_axis=0)
        places.append(jnp.sum(x, axis=0, keepdims=True))
    place = jnp.concatenate(places, axis=1).astype(jnp.int32)
    landing = jnp.where(iota((cells, slots), 0) + 1 == place, 1.0, 0.0)
    return selected(landing, jnp.concatenate([rows_of[part] for part in range(parts)], axis=1))


def land(room, chunk, got_ref, force, rows_of):
    rows, cols, _ = force.shape
    force[...] = landed(room, chunk, rows * cols, got_ref, rows_of).reshape(force.shape)


def tissue_steps(force, free, after_free, quarter, up, down, left, right, mid, new):
    rows = force.shape[0]

    def step(i, f_up, f_down):
        f = force[i]
        at = lambda ref: ref[pl.ds(i, 1), :]
        lap = f_up + f_down + beside(f, at(left), at(right)) + lateral(f) - 6.0 * f
        mid[i] = free[i] + 0.25 * f
        new[i] = after_free[i] + 0.75 * f + quarter[i] * lap

    step(0, up[...], force[1])
    step(rows - 1, force[rows - 2], down[...])

    def body(i, carry):
        step(i, force[i - 1], force[i + 1])
        return carry

    lax.fori_loop(1, rows - 1, body, 0)


def land_and_step(
    room, chunk, got_ref, free, after_free, quarter, force_out, mid_out, new_out,
    rows_of, field, mid, new, sems
):
    rows, cols, depth = mid.shape
    cells, parts = rows * cols, depth // 128
    x = landed(room, chunk, cells + 2 * (rows + cols), got_ref, rows_of)
    inside, copies = slice(8, 8 + cols), []
    for part in range(parts):
        lanes = slice(part * 128, part * 128 + 128)
        border = lambda start, size: x[cells + start : cells + start + size, lanes]
        field[0, part, inside, :] = border(0, cols)
        field[1 : rows + 1, part, inside, :] = x[:cells, lanes].reshape(rows, cols, 128)
        field[rows + 1, part, inside, :] = border(cols, cols)
        field[1 : rows + 1, part, 7, :] = border(2 * cols, rows)
        field[1 : rows + 1, part, 8 + cols, :] = border(2 * cols + rows, rows)
        copies.append(
            pltpu.make_async_copy(
                field.at[pl.ds(1, rows), part, pl.ds(8, cols), :],
                force_out.at[:, :, pl.ds(part * 128, 128)],
                sems.at[part],
            )
        )
        copies[-1].start()

    def step(i, carry):
        at = lambda row, part, start: field[row, part, start : start + cols, :]
        tiles = [at(i + 1, part, 8) for part in range(parts)]
        lane = iota(tiles[0].shape, 1)
        lower = [0.0] + [pltpu.roll(tile, 1, 1) for tile in tiles]
        upper = [pltpu.roll(tile, 127, 1) for tile in tiles] + [0.0]
        for part, f in enumerate(tiles):
            lanes = slice(part * 128, part * 128 + 128)
            lap = at(i, part, 8) + at(i + 2, part, 8) + at(i + 1, part, 7) + at(i + 1, part, 9)
            lap = lap + jnp.where(lane == 0, lower[part], lower[part + 1])
            lap = lap + jnp.where(lane == 127, upper[part + 1], upper[part]) - 6.0 * f
            mid[i, :, lanes] = free[i, :, lanes] + 0.25 * f
            new[i, :, lanes] = after_free[i, :, lanes] + 0.75 * f + quarter[i, :, lanes] * lap
        return carry

    pieces = (sems.shape[0] - parts) // 2
    for piece in range(pieces):
        first, last = rows * piece // pieces, rows * (piece + 1) // pieces
        lax.fori_loop(first, last, step, 0)
        part = pl.ds(first, last - first)
        for k, (ref, out) in enumerate(((mid, mid_out), (new, new_out))):
            sem = sems.at[parts + 2 * piece + k]
            copies.append(pltpu.make_async_copy(ref.at[part], out.at[part], sem))
            copies[-1].start()
    for copy in copies:
        copy.wait()


def far(*arrays):
    return [pltpu.with_memory_space_constraint(x, pltpu.HBM) for x in arrays]


def swap(first, last, axis):
    size = lax.axis_size(axis)
    up = [(i, i + 1) for i in range(size - 1)]
    down = [(j, i) for i, j in up]
    return lax.ppermute(last, axis, up), lax.ppermute(first, axis, down)


def local(
    pressure,
    pressure_prev,
    courant,
    nonlinearity,
    absorption,
    own_map,
    slot_table,
    displacement,
    displacement_prev,
    layer_labels,
    shear_table,
    viscosity_table,
):
    deep, across, span = pressure.shape
    rows, cols, depth = displacement.shape
    f32 = lambda *shape: jax.ShapeDtypeStruct(shape, jnp.float32)
    hbm = lambda *shape: pltpu.HBM(shape, jnp.float32)
    scratch = lambda *shape: pltpu.VMEM(shape, jnp.float32)

    def run(kernel, out, *args, scratch_shapes=(), tables=(), weight=1, limit=8):
        specs = [SMEM if k in tables else VMEM for k in range(len(args))]
        moved = weight * 4 * sum(math.prod(x.shape) for x in args + tuple(jax.tree.leaves(out)))
        cost = pl.CostEstimate(flops=20 * moved, bytes_accessed=moved, transcendentals=0)
        return pl.pallas_call(
            kernel,
            out_shape=out,
            in_specs=specs,
            out_specs=jax.tree.map(lambda _: VMEM, out),
            scratch_shapes=scratch_shapes,
            compiler_params=pltpu.CompilerParams(vmem_limit_bytes=limit << 20),
            cost_estimate=cost,
        )(*args)

    fields = (
        (pressure, 1),
        (pressure_prev, 0),
        (courant, 0),
        (nonlinearity, 0),
        (absorption, 0),
        (displacement, 1),
        (displacement_prev, 1),
        (layer_labels, 0),
    )
    arrays, inner = [x for x, _ in fields], [more for _, more in fields]
    side = 3 * deep + 2 * rows
    buffers = [
        pltpu.VMEM((x.shape[0], x.shape[2]), x.dtype)
        for x, more in fields
        for _ in range(2 * (1 + more))
    ]
    near = pl.BlockSpec(memory_space=pltpu.HBM)
    first, last = pl.pallas_call(
        functools.partial(border_columns, inner),
        out_shape=(pltpu.VMEM((side, span), jnp.float32),) * 2,
        in_specs=[near] * len(fields) + [SMEM, SMEM],
        out_specs=(VMEM, VMEM),
        scratch_shapes=buffers + [pltpu.SemaphoreType.DMA((len(buffers),))],
        compiler_params=pltpu.CompilerParams(vmem_limit_bytes=40 << 20),
    )(*far(*arrays, shear_table, viscosity_table))
    left, right = swap(first, last, "gy")
    pause = pl.pallas_call(
        cover,
        out_shape=f32(8, 128),
        in_specs=[pl.BlockSpec(memory_space=pl.ANY)],
        out_specs=VMEM,
        compiler_params=pltpu.CompilerParams(vmem_limit_bytes=1 << 20),
        cost_estimate=pl.CostEstimate(flops=2 * 10**10, bytes_accessed=10**9, transcendentals=0),
    )(first)
    block, tissue = f32(deep, across, span), f32(rows, cols, depth)
    mid, free = run(
        first_steps,
        (block, tissue),
        *arrays,
        shear_table,
        viscosity_table,
        pause,
        tables=(8, 9),
    )
    first, last = run(
        border_rows,
        (f32(3 * across + 2 * cols + 8, span),) * 2,
        pressure,
        courant,
        mid,
        displacement,
        displacement_prev,
        layer_labels,
        free,
        shear_table,
        viscosity_table,
        left,
        right,
        tables=(7, 8),
    )
    before, after = swap(first, last, "gx")
    grid = (lax.axis_size("gx"), lax.axis_size("gy"))
    blocks = grid[0] * grid[1]
    capacity = max(2, deep // 2 * (across // 2) // blocks)
    parts = depth // 128
    room = 2 * capacity + 1
    chunk = -(-(room * parts + 1) // 8) * 8
    count = own_map.size
    match, placed = pl.pallas_call(
        functools.partial(address, grid, (rows, cols), room, chunk),
        out_shape=(f32(blocks * chunk, parts * count), f32(blocks * chunk, 128)),
        in_specs=[VMEM, VMEM, pl.BlockSpec(memory_space=pl.ANY)],
        out_specs=(VMEM, VMEM),
        compiler_params=pltpu.CompilerParams(vmem_limit_bytes=16 << 20),
        cost_estimate=pl.CostEstimate(flops=10**8, bytes_accessed=10**7, transcendentals=0),
    )(own_map.T, slot_table.T, first)
    media = (pressure, courant, nonlinearity, absorption)
    mid, new, lines = run(
        second_acoustic,
        (block, block, f32(parts * count, 128)),
        *media,
        mid,
        left,
        right,
        scratch_shapes=[
            scratch(deep, span),
            scratch(deep, span),
            scratch(span // 128, deep // 2 * across, 128),
        ],
    )
    mids, news, send = run(
        ends_and_send,
        (hbm(2, across, span), hbm(4, across, span), hbm(blocks * chunk, 128)),
        *media,
        mid,
        lines,
        match,
        placed,
        before,
        after,
        left,
        right,
        scratch_shapes=[scratch(parts * count, 128), scratch(span // 128, across, 128)],
    )
    send = send.reshape(blocks, chunk, 128)
    got = lax.all_to_all(send, ("gx", "gy"), split_axis=0, concat_axis=0, tiled=True)
    pressure_mid, pressure_new, free, after_free, quarter = run(
        second_elastic,
        (block, block, tissue, tissue, tissue),
        *far(mid, new, mids, news, free, displacement, displacement_prev, layer_labels),
        shear_table,
        viscosity_table,
        *far(before, after, left, right),
        scratch_shapes=[scratch(rows, depth)] * 4,
        tables=(8, 9),
        limit=24,
    )
    slot = 8
    while slot < room:
        slot *= 2
    arrived = scratch(parts, blocks * slot, 128)

    def direct(got, *rest):
        return pl.pallas_call(
            functools.partial(land_and_step, room, chunk),
            out_shape=(hbm(rows, cols, depth),) * 3,
            in_specs=[VMEM] * 4,
            out_specs=(near,) * 3,
            scratch_shapes=[
                arrived,
                scratch(rows + 2, parts, cols + 16, 128),
                scratch(rows, cols, depth),
                scratch(rows, cols, depth),
                pltpu.SemaphoreType.DMA((parts + 8,)),
            ],
            compiler_params=pltpu.CompilerParams(vmem_limit_bytes=24 << 20),
        )(got, *rest)

    def by_faces(got, *rest):
        force = run(functools.partial(land, room, chunk), tissue, got, scratch_shapes=[arrived])
        up, down = swap(force[0], force[rows - 1], "gx")
        at_left, at_right = swap(force[:, 0], force[:, cols - 1], "gy")
        mid, new = run(
            tissue_steps, (tissue,) * 2, force, *rest, up, down, at_left, at_right, limit=16
        )
        return force, mid, new

    tissue_force, displacement_mid, displacement_new = lax.cond(
        jnp.max(got[:, chunk - 1, room]) > 0.0,
        by_faces,
        direct,
        got.reshape(blocks * chunk, 128),
        free,
        after_free,
        quarter,
    )
    return (pressure_mid, pressure_new, tissue_force, displacement_mid, displacement_new)


def solution(mesh):
    block = P(("group", "gx"), "gy", None)
    plane = P(("group", "gx"), "gy")
    return jax.shard_map(
        local,
        mesh=mesh,
        in_specs=(block,) * 5 + (plane,) * 2 + (block,) * 3 + (P("group"),) * 2,
        out_specs=(block,) * 5,
        check_vma=False,
    )
```

```python
import functools
import math

import jax
import jax.numpy as jnp
from jax import lax
from jax.experimental import pallas as pl
from jax.experimental.pallas import tpu as pltpu
from jax.sharding import PartitionSpec as P

VMEM = pl.BlockSpec(memory_space=pltpu.VMEM)
SMEM = pl.BlockSpec(memory_space=pltpu.SMEM)
EXACT = lax.Precision.HIGHEST


def lateral(x):
    tiles = [x[:, at : at + 128] for at in range(0, x.shape[1], 128)]
    lane = lax.broadcasted_iota(jnp.int32, tiles[0].shape, 1)
    lower = [0.0] + [pltpu.roll(tile, 1, 1) for tile in tiles]
    upper = [pltpu.roll(tile, 127, 1) for tile in tiles] + [0.0]
    sums = [
        jnp.where(lane == 0, lower[k], lower[k + 1])
        + jnp.where(lane == 127, upper[k + 1], upper[k])
        for k in range(len(tiles))
    ]
    return jnp.concatenate(sums, axis=1)


def beside(x, before, after):
    tiles = [x[at : at + 8] for at in range(0, x.shape[0], 8)]
    row = lax.broadcasted_iota(jnp.int32, tiles[0].shape, 0)
    up = [before] + [pltpu.roll(tile, 1, 0) for tile in tiles]
    down = [pltpu.roll(tile, 7, 0) for tile in tiles] + [after]
    sums = [
        jnp.where(row == 0, up[k], up[k + 1]) + jnp.where(row == 7, down[k + 1], down[k])
        for k in range(len(tiles))
    ]
    return jnp.concatenate(sums, axis=0)


class Facing:
    def __init__(self, odd, at_even, at_odd):
        self.odd, self.at_even, self.at_odd = odd, at_even, at_odd
        self.shape = at_even.shape

    def __getitem__(self, at):
        return jnp.where(self.odd, self.at_odd[at], self.at_even[at])


def facing(axis, inner, outer):
    odd = lax.rem(lax.axis_index(axis), 2) == 1
    return Facing(odd, outer, inner), Facing(odd, inner, outer)


def by_parity(axis, both, inner, outer):
    odd = lax.rem(lax.axis_index(axis), 2)
    inner[...] = both[1 - odd]
    outer[...] = both[odd]


def at_ends(shape, first, last):
    row = lax.broadcasted_iota(jnp.int32, shape, 0)
    return jnp.where(row == 0, first, jnp.where(row == shape[0] - 1, last, 0.0))


def wave(now, before, lap, courant, nonlinearity, absorption):
    return (
        2.0 * now
        - before
        + courant * lap
        + nonlinearity * (now * now - before * before)
        - 0.1 * absorption * (now - before)
    )


def lookup(kinds, table, first):
    values = [table[kind] for kind in range(len(table) if isinstance(table, list) else table.shape[0])]
    result = jnp.full(kinds.shape, 0.0 if first else values[0], jnp.float32)
    for kind in range(0 if first else 1, len(values)):
        result = jnp.where(kinds == kind + first, values[kind], result)
    return result


def halves(ref, base, x):
    half, depth = x.shape[0] // 2, x.shape[1]
    ref[base : base + half, 0:depth] = x[:half]
    ref[base : base + half, depth : 2 * depth] = x[half:]


def whole(ref, base, half, depth):
    return jnp.concatenate(
        [ref[base : base + half, 0:depth], ref[base : base + half, depth : 2 * depth]], axis=0
    )


def border_columns(inner, *refs):
    count = len(inner)
    fields, (shear, viscosity, inner_out, outer_out) = refs[:count], refs[count : count + 4]
    buffers, both, sems = refs[count + 4 : -2], refs[-2], refs[-1]
    left, right = both.at[0], both.at[1]
    groups, k = [], 0
    for some in (range(0, 5), range(5, count)):
        for side in range(2):
            group = []
            for field in some:
                last = fields[field].shape[1] - 1
                for step in range(1 + inner[field]):
                    j = last - step if side else step
                    source = fields[field].at[:, j, :]
                    copy = pltpu.make_async_copy(source, buffers[k], sems.at[k])
                    copy.start()
                    group.append((copy, buffers[k]))
                    k += 1
            groups.append(group)

    def columns(group):
        for copy, _ in group:
            copy.wait()
        return [buffer[...] for _, buffer in group]

    for group, out in zip(groups[:2], (left, right)):
        p, p_in, q, c, n, a = columns(group)
        deep = p.shape[0]
        lap = beside(p, 0.0, 0.0) + p_in + lateral(p) - 6.0 * p
        out[0:deep] = p
        out[deep : 2 * deep] = c
        out[2 * deep : 3 * deep] = wave(p, q, lap, c, n, a)
    top = 3 * deep
    for group, out in zip(groups[2:], (left, right)):
        d, d_in, b, b_in, labels = columns(group)
        rows, depth = d.shape
        e, e_in = d - b, d_in - b_in
        s, v = lookup(labels, shear, 0), lookup(labels, viscosity, 0)
        lap_d = beside(d, 0.0, 0.0) + d_in + lateral(d) - 6.0 * d
        lap_e = beside(e, 0.0, 0.0) + e_in + lateral(e) - 6.0 * e
        first, last = slice(0, depth), slice(depth, 2 * depth)
        out[top : top + rows, first] = d
        out[top : top + rows, last] = e
        out[top + rows : top + 2 * rows, first] = labels.astype(jnp.float32) + 1.0
        out[top + rows : top + 2 * rows, last] = d + e + s * lap_d + v * lap_e
    by_parity("gy", both, inner_out, outer_out)


def cover(_, out):
    out[...] = jnp.zeros_like(out)


def first_steps(p_ref, q_ref, c_ref, n_ref, a_ref, d_ref, b_ref, l_ref, shear, viscosity, _, mid, free):
    deep, rows = p_ref.shape[0], d_ref.shape[0]

    def acoustic(i, p_up, p_down):
        p = p_ref[i]
        lap = p_up + p_down + beside(p, 0.0, 0.0) + lateral(p) - 6.0 * p
        mid[i] = wave(p, q_ref[i], lap, c_ref[i], n_ref[i], a_ref[i])

    acoustic(0, 0.0, p_ref[1])
    acoustic(deep - 1, p_ref[deep - 2], 0.0)

    def acoustic_body(i, carry):
        acoustic(i, p_ref[i - 1], p_ref[i + 1])
        return carry

    lax.fori_loop(1, deep - 1, acoustic_body, 0)

    def elastic(i, d_up, d_down, e_up, e_down):
        d = d_ref[i]
        e = d - b_ref[i]
        s, v = lookup(l_ref[i], shear, 0), lookup(l_ref[i], viscosity, 0)
        lap_d = d_up + d_down + beside(d, 0.0, 0.0) + lateral(d) - 6.0 * d
        lap_e = e_up + e_down + beside(e, 0.0, 0.0) + lateral(e) - 6.0 * e
        free[i] = d + e + s * lap_d + v * lap_e

    change = lambda i: d_ref[i] - b_ref[i]
    elastic(0, 0.0, d_ref[1], 0.0, change(1))
    elastic(rows - 1, d_ref[rows - 2], 0.0, change(rows - 2), 0.0)

    def elastic_body(i, carry):
        elastic(i, d_ref[i - 1], d_ref[i + 1], change(i - 1), change(i + 1))
        return carry

    lax.fori_loop(1, rows - 1, elastic_body, 0)


def border_rows(
    p_ref, c_ref, mid_ref, d_ref, b_ref, l_ref, free_ref, shear, viscosity, beside_in, beside_out,
    inner_out, outer_out, both
):
    left, right = facing("gy", beside_in, beside_out)
    up, down = both.at[0], both.at[1]
    deep, across, _ = p_ref.shape
    rows, cols, depth = d_ref.shape
    half = cols // 2
    top, base, end = 3 * deep, 3 * across, 3 * across + 2 * cols
    first, last = slice(0, depth), slice(depth, 2 * depth)
    for i, k, out in ((0, 0, up), (deep - 1, rows - 1, down)):
        p, c = p_ref[i], c_ref[i]
        p_left, p_right = left[i : i + 1], right[i : i + 1]
        out[0:across] = p
        out[across : 2 * across] = c
        out[2 * across : 3 * across] = mid_ref[i] + c * at_ends(c.shape, p_left, p_right)
        d, labels = d_ref[k], l_ref[k]
        s, v = lookup(labels, shear, 0), lookup(labels, viscosity, 0)
        at = slice(top + k, top + k + 1)
        d_ends = at_ends(d.shape, left[at, first], right[at, first])
        e_ends = at_ends(d.shape, left[at, last], right[at, last])
        halves(out, base, d)
        halves(out, base + half, d - b_ref[k])
        halves(out, base + 2 * half, free_ref[k] + s * d_ends + v * e_ends)
        halves(out, base + 3 * half, labels.astype(jnp.float32) + 1.0)
        out[end : end + 1] = p_left
        out[end + 1 : end + 2] = p_right
        out[end + 2 : end + 3] = left[at]
        out[end + 3 : end + 4] = right[at]
        out[end + 4 : end + 8] = jnp.zeros((4, out.shape[1]), jnp.float32)
    by_parity("gx", both, inner_out, outer_out)


def dot(x, y, contract=((1,), (0,))):
    return lax.dot_general(
        x, y, (contract, ((), ())), precision=EXACT, preferred_element_type=jnp.float32
    )


def selected(x, y):
    high = y.astype(jnp.bfloat16)
    low = (y - high.astype(jnp.float32)).astype(jnp.bfloat16)
    x = x.astype(jnp.bfloat16)
    product = functools.partial(jnp.dot, preferred_element_type=jnp.float32)
    return product(x, high) + product(x, low)


def iota(shape, dim):
    return lax.broadcasted_iota(jnp.int32, shape, dim)


def address(grid, tile, room, chunk, own_ref, slot_ref, _, match, ends, placed):
    (tiles_down, tiles_across), (rows, cols) = grid, tile
    blocks, cells = tiles_down * tiles_across, rows * cols
    wide, tall = own_ref.shape
    count = wide * tall
    parts = match.shape[1] // count

    spread = (iota((tall, count), 1) // wide == iota((tall, count), 0)).astype(jnp.float32)
    mine = iota((wide, count), 1) % wide == iota((wide, count), 0)
    spread_t = (iota((count, tall), 0) // wide == iota((count, tall), 1)).astype(jnp.float32)
    mine_t = iota((count, wide), 0) % wide == iota((count, wide), 1)

    def flat(ref):
        x = ref[...].astype(jnp.float32)
        along = jnp.sum(jnp.where(mine, dot(x, spread), 0.0), axis=0, keepdims=True)
        down = dot(spread_t, x, ((1,), (1,)))
        down = jnp.sum(jnp.where(mine_t, down, 0.0), axis=1, keepdims=True)
        return along.astype(jnp.int32), down.astype(jnp.int32)

    def entries(own, slot):
        r, c = slot // cols, slot % cols
        tile_r, tile_c = own // tiles_across, own % tiles_across
        focal = own < blocks
        nobody = jnp.full(own.shape, -1, jnp.int32)
        up = focal & (r == 0) & (tile_r > 0)
        down = focal & (r == rows - 1) & (tile_r < tiles_down - 1)
        left = focal & (c == 0) & (tile_c > 0)
        right = focal & (c == cols - 1) & (tile_c < tiles_across - 1)
        to = (
            jnp.where(focal, own, nobody),
            jnp.where(up, own - tiles_across, jnp.where(down, own + tiles_across, nobody)),
            jnp.where(left, own - 1, jnp.where(right, own + 1, nobody)),
        )
        place = (
            slot,
            cells + c + jnp.where(up, cols, 0),
            cells + 2 * cols + r + jnp.where(left, rows, 0),
        )
        return to, place

    (own_row, own_col), (slot_row, slot_col) = flat(own_ref), flat(slot_ref)
    to_row, place_row = entries(own_row, slot_row)
    to_col, _ = entries(own_col, slot_col)
    ones = lambda x: jnp.where(x, 1.0, 0.0)
    earlier = iota((count, count), 0) < iota((count, count), 1)
    used, ranks = jnp.zeros(own_row.shape, jnp.float32), []
    for k in range(3):
        rank = jnp.zeros(own_row.shape, jnp.float32)
        for other in range(k + 1):
            same = to_col[other] == to_row[k]
            same = same & earlier if other == k else same
            rank = rank + jnp.sum(ones(same), axis=0, keepdims=True)
        ranks.append(rank.astype(jnp.int32))
        used = jnp.maximum(used, jnp.where(to_row[k] >= 0, rank + 1.0, 0.0))
    full = jnp.where(jnp.max(used) > room, 1.0, 0.0)
    total = blocks * chunk
    at = iota((total, count), 0)
    fits = [(to >= 0) & (rank < room) for to, rank in zip(to_row, ranks)]
    base = [
        jnp.where(fit, to * chunk + rank, -total) for fit, to, rank in zip(fits, to_row, ranks)
    ]
    for part in range(parts):
        here = at - part * room
        one_hot = sum(ones(here == b) for b in base).astype(jnp.bfloat16)
        match[:, part * count : part * count + count] = one_hot
        for k, lines in enumerate((slice(0, wide), slice(count - wide, count))):
            first = (2 * part + k) * wide
            ends[:, first : first + wide] = one_hot[:, lines]
    lanes = (128, count)
    row, lane = iota((total, 128), 0), iota((total, 128), 1)
    result = jnp.where((row % chunk == chunk - 1) & (lane == room), full, 0.0)
    for fit, to, rank, place in zip(fits, to_row, ranks, place_row):
        target = ones(at == jnp.where(fit, to * chunk + chunk - 1, -1))
        value = jnp.where(iota(lanes, 0) == rank, place.astype(jnp.float32) + 1.0, 0.0)
        result = result + dot(target, value, ((1,), (1,)))
    placed[...] = result


def radiated(m, new, courant, absorption):
    return 0.1 * absorption * (m * m + new * new) * lax.rsqrt(courant)


def paired_lanes(x):
    pairing = iota((256, 128), 0) // 2 == iota((256, 128), 1)
    pairing = pairing.astype(jnp.float32).astype(jnp.bfloat16)
    high = x.astype(jnp.bfloat16)
    low = (x - high.astype(jnp.float32)).astype(jnp.bfloat16)
    product = functools.partial(jnp.dot, preferred_element_type=jnp.float32)
    return [
        product(high[:, at : at + 256], pairing) + product(low[:, at : at + 256], pairing)
        for at in range(0, x.shape[1], 256)
    ]


def even_and_odd(ref, count):
    return jnp.concatenate(
        [
            ref[part, pl.ds(0, count, stride=2), :] + ref[part, pl.ds(1, count, stride=2), :]
            for part in range(ref.shape[0])
        ],
        axis=1,
    )


def step_rows(i, m, up, down, first, last, p_ref, c_ref, n_ref, a_ref):
    c, a = c_ref[i], a_ref[i]
    lap = up + down + beside(m, first, last) + lateral(m) - 6.0 * m
    new = wave(m, p_ref[i], lap, c, n_ref[i], a)
    return new, radiated(m, new, c, a)


def put(ref, start, value):
    for part in range(ref.shape[0]):
        ref[part, pl.ds(start, value.shape[0]), :] = value[:, part * 128 : part * 128 + 128]


def second_acoustic(
    p_ref, c_ref, n_ref, a_ref, mid_ref, match_ref, placed_ref, beside_in, beside_out,
    mid, new, send, beyond_l, beyond_r, pairs
):
    left, right = facing("gy", beside_in, beside_out)
    deep, across, _ = p_ref.shape
    mid[...] = mid_ref[...]
    for j, side, beyond in ((0, left, beyond_l), (across - 1, right, beyond_r)):
        mid[:, j, :] = mid_ref[:, j, :] + c_ref[:, j, :] * side[0:deep]
        beyond[...] = side[2 * deep : 3 * deep] + side[deep : 2 * deep] * p_ref[:, j, :]

    def body(k, carry):
        i = 2 * k
        total = 0.0
        for at in (i, i + 1):
            one = pl.ds(at, 1)
            result, force = step_rows(
                at, mid[at], mid[at - 1], mid[at + 1], beyond_l[one, :], beyond_r[one, :],
                p_ref, c_ref, n_ref, a_ref,
            )
            new[at] = result
            total = total + force
        put(pairs, pl.multiple_of(k * across, across), total)
        return carry

    for at in (0, 1, deep - 2, deep - 1):
        new[at] = jnp.zeros(new.shape[1:], jnp.float32)
    put(pairs, 0, jnp.zeros(new.shape[1:], jnp.float32))
    put(pairs, (deep // 2 - 1) * across, jnp.zeros(new.shape[1:], jnp.float32))
    lax.fori_loop(1, deep // 2 - 1, body, 0)
    lines = paired_lanes(even_and_odd(pairs, deep // 2 * (across // 2)))
    send[...] = selected(match_ref[...], 0.125 * jnp.concatenate(lines, axis=0)) + placed_ref[...]


def ends_and_send(
    p_ref, c_ref, n_ref, a_ref, mid_ref, sent_ref, ends_ref,
    beside_in, beside_out, near_in, near_out, mids, news, send, pairs
):
    left, right = facing("gy", beside_in, beside_out)
    before, after = facing("gx", near_in, near_out)
    deep, across, _ = p_ref.shape
    cols = (before.shape[0] - 8 - 3 * across) // 2
    corners = 3 * across + 2 * cols
    media = (p_ref, c_ref, n_ref, a_ref)

    def beyond(side, j, i):
        return side[2 * deep + i : 2 * deep + i + 1] + side[deep + i : deep + i + 1] * p_ref[
            i, j : j + 1, :
        ]

    lines = []
    for k, (i, inner, more, side) in enumerate(
        ((0, 1, 2, before), (deep - 1, deep - 2, deep - 3, after))
    ):
        m = mid_ref[i] + c_ref[i] * side[0:across]
        m_in = mid_ref[inner]
        outer = side[2 * across : 3 * across] + side[across : 2 * across] * p_ref[i]
        first = beyond(left, 0, i) + left[deep + i : deep + i + 1] * side[corners : corners + 1]
        last = (
            beyond(right, across - 1, i)
            + right[deep + i : deep + i + 1] * side[corners + 1 : corners + 2]
        )
        new, force = step_rows(i, m, outer, m_in, first, last, *media)
        first, last = beyond(left, 0, inner), beyond(right, across - 1, inner)
        new_in, force_in = step_rows(inner, m_in, m, mid_ref[more], first, last, *media)
        mids[k] = m
        news[2 * k] = new
        news[2 * k + 1] = new_in
        put(pairs, k * across, force + force_in)
    half = across // 2
    lines = paired_lanes(even_and_odd(pairs, 2 * half))
    send[...] = sent_ref[...] + selected(ends_ref[...], 0.125 * jnp.concatenate(lines, axis=0))


def second_elastic(
    mid_ref, new_ref, mids, news, free_ref, d_ref, b_ref, l_ref, shear, viscosity,
    beside_in, beside_out, near_in, near_out,
    mid, new, free, after_free, quarter, d_first, d_last, f_first, f_last
):
    left, right = facing("gy", beside_in, beside_out)
    before, after = facing("gx", near_in, near_out)
    deep, across, _ = mid.shape
    mid[...] = mid_ref[...]
    new[...] = new_ref[...]
    for k, (i, inner) in enumerate(((0, 1), (deep - 1, deep - 2))):
        mid[i] = mids[k]
        new[i] = news[2 * k]
        new[inner] = news[2 * k + 1]
    rows, cols, depth = d_ref.shape
    half = cols // 2
    top, base, corners = 3 * deep, 3 * across, 3 * across + 2 * cols
    lanes, others = slice(0, depth), slice(depth, 2 * depth)
    free[...] = free_ref[...]
    for i, side in ((0, before), (rows - 1, after)):
        s, v = lookup(l_ref[i], shear, 0), lookup(l_ref[i], viscosity, 0)
        free[i] = (
            free_ref[i]
            + s * whole(side, base, half, depth)
            + v * whole(side, base + half, half, depth)
        )
    now, then = slice(top, top + rows), slice(top + rows, top + 2 * rows)
    for k, (j, side, d_col, f_col) in enumerate(
        ((0, left, d_first, f_first), (cols - 1, right, d_last, f_last))
    ):
        labels = l_ref[:, j, :]
        s, v = lookup(labels, shear, 0), lookup(labels, viscosity, 0)
        d_side, e_side = side[now, lanes], side[now, others]
        free[:, j, :] = free[:, j, :] + s * d_side + v * e_side
        kinds = side[then, lanes]
        s, v = lookup(kinds, shear, 1.0), lookup(kinds, viscosity, 1.0)
        d = d_ref[:, j, :]
        at = slice(corners + 2 + k, corners + 3 + k)
        d_ends = at_ends(d.shape, before[at, lanes], after[at, lanes])
        e_ends = at_ends(d.shape, before[at, others], after[at, others])
        d_col[...] = d_side
        f_col[...] = side[then, others] + s * (d + d_ends) + v * (d - b_ref[:, j, :] + e_ends)

    def beyond(side, edge):
        part = lambda n: whole(side, base + n * half, half, depth)
        d, kinds = part(0), part(3)
        s, v = lookup(kinds, shear, 1.0), lookup(kinds, viscosity, 1.0)
        d_edge = d_ref[edge]
        return part(2) + s * d_edge + v * (d_edge - b_ref[edge]), d

    def step(i, f_up, f_down, d_up, d_down):
        f, d = free[i], d_ref[i]
        s, v = lookup(l_ref[i], shear, 0), lookup(l_ref[i], viscosity, 0)
        at = lambda ref: ref[pl.ds(i, 1), :]
        lap_f = f_up + f_down + beside(f, at(f_first), at(f_last)) + lateral(f) - 6.0 * f
        lap_d = d_up + d_down + beside(d, at(d_first), at(d_last)) + lateral(d) - 6.0 * d
        after_free[i] = 2.0 * f - d + s * lap_f + v * (lap_f - lap_d)
        quarter[i] = 0.25 * (s + v)

    f_up, d_up = beyond(before, 0)
    step(0, f_up, free[1], d_up, d_ref[1])
    f_down, d_down = beyond(after, rows - 1)
    step(rows - 1, free[rows - 2], f_down, d_ref[rows - 2], d_down)

    def body(i, carry):
        step(i, free[i - 1], free[i + 1], d_ref[i - 1], d_ref[i + 1])
        return carry

    lax.fori_loop(1, rows - 1, body, 0)


def landed(room, chunk, cells, got_ref, rows_of):
    total = got_ref.shape[0]
    parts, slots, _ = rows_of.shape
    blocks = total // chunk
    slot = slots // blocks
    for source in range(blocks):
        for part in range(parts):
            start = source * chunk + part * room
            size = min(slot, total - start)
            at = source * slot
            rows_of[part, at : at + size, :] = got_ref[start : start + size, :]
            if size < slot:
                rows_of[part, at + size : at + slot, :] = jnp.zeros((slot - size, 128), jnp.float32)
    places, group = [], 128 // slot
    for first in range(0, blocks, group):
        x = got_ref[pl.ds(first * chunk + chunk - 1, group, stride=chunk), :]
        x = jnp.where(iota(x.shape, 1) < room, x, 0.0)
        x = pltpu.roll(x, 0, 1, stride=slot, stride_axis=0)
        places.append(jnp.sum(x, axis=0, keepdims=True))
    place = jnp.concatenate(places, axis=1).astype(jnp.int32)
    landing = jnp.where(iota((cells, slots), 0) + 1 == place, 1.0, 0.0)
    return selected(landing, jnp.concatenate([rows_of[part] for part in range(parts)], axis=1))


def land(room, chunk, got_ref, force, rows_of):
    rows, cols, _ = force.shape
    force[...] = landed(room, chunk, rows * cols, got_ref, rows_of).reshape(force.shape)


def tissue_steps(force, free, after_free, quarter, up, down, left, right, mid, new):
    rows = force.shape[0]

    def step(i, f_up, f_down):
        f = force[i]
        at = lambda ref: ref[pl.ds(i, 1), :]
        lap = f_up + f_down + beside(f, at(left), at(right)) + lateral(f) - 6.0 * f
        mid[i] = free[i] + 0.25 * f
        new[i] = after_free[i] + 0.75 * f + quarter[i] * lap

    step(0, up[...], force[1])
    step(rows - 1, force[rows - 2], down[...])

    def body(i, carry):
        step(i, force[i - 1], force[i + 1])
        return carry

    lax.fori_loop(1, rows - 1, body, 0)


def land_and_step(
    room, chunk, got_ref, free, after_free, quarter, force_out, mid_out, new_out,
    rows_of, field, mid, new, sems
):
    rows, cols, depth = mid.shape
    cells, parts = rows * cols, depth // 128
    x = landed(room, chunk, cells + 2 * (rows + cols), got_ref, rows_of)
    inside, copies = slice(8, 8 + cols), []
    for part in range(parts):
        lanes = slice(part * 128, part * 128 + 128)
        border = lambda start, size: x[cells + start : cells + start + size, lanes]
        field[0, part, inside, :] = border(0, cols)
        field[1 : rows + 1, part, inside, :] = x[:cells, lanes].reshape(rows, cols, 128)
        field[rows + 1, part, inside, :] = border(cols, cols)
        field[1 : rows + 1, part, 7, :] = border(2 * cols, rows)
        field[1 : rows + 1, part, 8 + cols, :] = border(2 * cols + rows, rows)
        copies.append(
            pltpu.make_async_copy(
                field.at[pl.ds(1, rows), part, pl.ds(8, cols), :],
                force_out.at[:, :, pl.ds(part * 128, 128)],
                sems.at[part],
            )
        )
        copies[-1].start()

    def step(i, carry):
        at = lambda row, part, start: field[row, part, start : start + cols, :]
        tiles = [at(i + 1, part, 8) for part in range(parts)]
        lane = iota(tiles[0].shape, 1)
        lower = [0.0] + [pltpu.roll(tile, 1, 1) for tile in tiles]
        upper = [pltpu.roll(tile, 127, 1) for tile in tiles] + [0.0]
        for part, f in enumerate(tiles):
            lanes = slice(part * 128, part * 128 + 128)
            lap = at(i, part, 8) + at(i + 2, part, 8) + at(i + 1, part, 7) + at(i + 1, part, 9)
            lap = lap + jnp.where(lane == 0, lower[part], lower[part + 1])
            lap = lap + jnp.where(lane == 127, upper[part + 1], upper[part]) - 6.0 * f
            mid[i, :, lanes] = free[i, :, lanes] + 0.25 * f
            new[i, :, lanes] = after_free[i, :, lanes] + 0.75 * f + quarter[i, :, lanes] * lap
        return carry

    pieces = (sems.shape[0] - parts) // 2
    for piece in range(pieces):
        first, last = rows * piece // pieces, rows * (piece + 1) // pieces
        lax.fori_loop(first, last, step, 0)
        part = pl.ds(first, last - first)
        for k, (ref, out) in enumerate(((mid, mid_out), (new, new_out))):
            sem = sems.at[parts + 2 * piece + k]
            copies.append(pltpu.make_async_copy(ref.at[part], out.at[part], sem))
            copies[-1].start()
    for copy in copies:
        copy.wait()


def far(*arrays):
    return [pltpu.with_memory_space_constraint(x, pltpu.HBM) for x in arrays]


def swap(first, last, axis):
    size = lax.axis_size(axis)
    up = [(i, i + 1) for i in range(size - 1)]
    down = [(j, i) for i, j in up]
    return lax.ppermute(last, axis, up), lax.ppermute(first, axis, down)


def swap_pairs(inner, outer, axis):
    size = lax.axis_size(axis)
    pairs = lambda first: [
        pair for i in range(first, size - 1, 2) for pair in ((i, i + 1), (i + 1, i))
    ]
    outer = lax.ppermute(outer, axis, pairs(1))
    return lax.ppermute(inner, axis, pairs(0)), outer


def local(
    pressure,
    pressure_prev,
    courant,
    nonlinearity,
    absorption,
    own_map,
    slot_table,
    displacement,
    displacement_prev,
    layer_labels,
    shear_table,
    viscosity_table,
):
    deep, across, span = pressure.shape
    rows, cols, depth = displacement.shape
    f32 = lambda *shape: jax.ShapeDtypeStruct(shape, jnp.float32)
    hbm = lambda *shape: pltpu.HBM(shape, jnp.float32)
    half = lambda *shape: jax.ShapeDtypeStruct(shape, jnp.bfloat16)
    scratch = lambda *shape: pltpu.VMEM(shape, jnp.float32)

    def run(kernel, out, *args, scratch_shapes=(), tables=(), weight=1, limit=8):
        specs = [SMEM if k in tables else VMEM for k in range(len(args))]
        moved = weight * 4 * sum(math.prod(x.shape) for x in args + tuple(jax.tree.leaves(out)))
        cost = pl.CostEstimate(flops=20 * moved, bytes_accessed=moved, transcendentals=0)
        return pl.pallas_call(
            kernel,
            out_shape=out,
            in_specs=specs,
            out_specs=jax.tree.map(lambda _: VMEM, out),
            scratch_shapes=scratch_shapes,
            compiler_params=pltpu.CompilerParams(vmem_limit_bytes=limit << 20),
            cost_estimate=cost,
        )(*args)

    fields = (
        (pressure, 1),
        (pressure_prev, 0),
        (courant, 0),
        (nonlinearity, 0),
        (absorption, 0),
        (displacement, 1),
        (displacement_prev, 1),
        (layer_labels, 0),
    )
    arrays, inner = [x for x, _ in fields], [more for _, more in fields]
    side = 3 * deep + 2 * rows
    buffers = [
        pltpu.VMEM((x.shape[0], x.shape[2]), x.dtype)
        for some in (fields[:5], fields[5:])
        for _ in range(2)
        for x, more in some
        for _ in range(1 + more)
    ]
    near = pl.BlockSpec(memory_space=pltpu.HBM)
    first, last = pl.pallas_call(
        functools.partial(border_columns, inner),
        out_shape=(pltpu.VMEM((side, span), jnp.float32),) * 2,
        in_specs=[near] * len(fields) + [SMEM, SMEM],
        out_specs=(VMEM, VMEM),
        scratch_shapes=buffers
        + [scratch(2, side, span), pltpu.SemaphoreType.DMA((len(buffers),))],
        compiler_params=pltpu.CompilerParams(vmem_limit_bytes=40 << 20),
    )(*far(*arrays, shear_table, viscosity_table))
    beside_sides = swap_pairs(first, last, "gy")
    pause = pl.pallas_call(
        cover,
        out_shape=f32(8, 128),
        in_specs=[pl.BlockSpec(memory_space=pl.ANY)],
        out_specs=VMEM,
        compiler_params=pltpu.CompilerParams(vmem_limit_bytes=1 << 20),
        cost_estimate=pl.CostEstimate(flops=2 * 10**10, bytes_accessed=10**9, transcendentals=0),
    )(first)
    block, tissue = f32(deep, across, span), f32(rows, cols, depth)
    mid, free = run(
        first_steps,
        (block, tissue),
        *arrays,
        shear_table,
        viscosity_table,
        pause,
        tables=(8, 9),
    )
    first, last = run(
        border_rows,
        (f32(3 * across + 2 * cols + 8, span),) * 2,
        pressure,
        courant,
        mid,
        displacement,
        displacement_prev,
        layer_labels,
        free,
        shear_table,
        viscosity_table,
        *beside_sides,
        scratch_shapes=[scratch(2, 3 * across + 2 * cols + 8, span)],
        tables=(7, 8),
    )
    near_sides = swap_pairs(first, last, "gx")
    grid = (lax.axis_size("gx"), lax.axis_size("gy"))
    blocks = grid[0] * grid[1]
    capacity = max(2, deep // 2 * (across // 2) // blocks)
    parts = depth // 128
    room = 2 * capacity + 1
    chunk = -(-(room * parts + 1) // 8) * 8
    count = own_map.size
    match, ends, placed = pl.pallas_call(
        functools.partial(address, grid, (rows, cols), room, chunk),
        out_shape=(
            half(blocks * chunk, parts * count),
            half(blocks * chunk, parts * across),
            f32(blocks * chunk, 128),
        ),
        in_specs=[VMEM, VMEM, pl.BlockSpec(memory_space=pl.ANY)],
        out_specs=(VMEM,) * 3,
        compiler_params=pltpu.CompilerParams(vmem_limit_bytes=16 << 20),
        cost_estimate=pl.CostEstimate(flops=10**8, bytes_accessed=10**7, transcendentals=0),
    )(own_map.T, slot_table.T, first)
    media = (pressure, courant, nonlinearity, absorption)
    mid, new, send = run(
        second_acoustic,
        (block, block, f32(blocks * chunk, 128)),
        *media,
        mid,
        match,
        placed,
        *beside_sides,
        scratch_shapes=[
            scratch(deep, span),
            scratch(deep, span),
            scratch(span // 128, deep // 2 * across, 128),
        ],
    )
    mids, news, send = run(
        ends_and_send,
        (hbm(2, across, span), hbm(4, across, span), hbm(blocks * chunk, 128)),
        *media,
        mid,
        send,
        ends,
        *beside_sides,
        *near_sides,
        scratch_shapes=[scratch(span // 128, 2 * across, 128)],
    )
    send = send.reshape(blocks, chunk, 128)
    got = lax.all_to_all(send, ("gx", "gy"), split_axis=0, concat_axis=0, tiled=True)
    pressure_mid, pressure_new, free, after_free, quarter = run(
        second_elastic,
        (block, block, tissue, tissue, tissue),
        *far(mid, new, mids, news, free, displacement, displacement_prev, layer_labels),
        shear_table,
        viscosity_table,
        *far(*beside_sides, *near_sides),
        scratch_shapes=[scratch(rows, depth)] * 4,
        tables=(8, 9),
        limit=24,
    )
    slot = 8
    while slot < room:
        slot *= 2
    arrived = scratch(parts, blocks * slot, 128)

    def direct(got, *rest):
        return pl.pallas_call(
            functools.partial(land_and_step, room, chunk),
            out_shape=(hbm(rows, cols, depth),) * 3,
            in_specs=[VMEM] * 4,
            out_specs=(near,) * 3,
            scratch_shapes=[
                arrived,
                scratch(rows + 2, parts, cols + 16, 128),
                scratch(rows, cols, depth),
                scratch(rows, cols, depth),
                pltpu.SemaphoreType.DMA((parts + 8,)),
            ],
            compiler_params=pltpu.CompilerParams(vmem_limit_bytes=24 << 20),
        )(got, *rest)

    def by_faces(got, *rest):
        force = run(functools.partial(land, room, chunk), tissue, got, scratch_shapes=[arrived])
        up, down = swap(force[0], force[rows - 1], "gx")
        at_left, at_right = swap(force[:, 0], force[:, cols - 1], "gy")
        mid, new = run(
            tissue_steps, (tissue,) * 2, force, *rest, up, down, at_left, at_right, limit=16
        )
        return force, mid, new

    tissue_force, displacement_mid, displacement_new = lax.cond(
        jnp.max(got[:, chunk - 1, room]) > 0.0,
        by_faces,
        direct,
        got.reshape(blocks * chunk, 128),
        free,
        after_free,
        quarter,
    )
    return (pressure_mid, pressure_new, tissue_force, displacement_mid, displacement_new)


def solution(mesh):
    block = P(("group", "gx"), "gy", None)
    plane = P(("group", "gx"), "gy")
    return jax.shard_map(
        local,
        mesh=mesh,
        in_specs=(block,) * 5 + (plane,) * 2 + (block,) * 3 + (P("group"),) * 2,
        out_specs=(block,) * 5,
        check_vma=False,
    )
```
